32 devices in a mesh: groups: 2 (over x), freq: 16 (over z, y, core).
Axes of the slice: x: 2, y: 2, z: 4, core: 2. Of those that a mesh axis runs over, the one named last changes fastest.
Arguments:
- voltages: bfloat16 [32, 263, 2, 2, 2048], P(('groups', 'freq')), parts along dimension 0, may hold values from -12 to 12
- pfb_taps: float32 [8, 2], replicated, may hold values from 0.2 to 1
- steering: bfloat16 [64, 2, 2048, 64], P(('groups', 'freq')), parts along dimension 0, may hold values from -0.09375 to 0.09375
- fdmt_offsets: int32 [5, 2, 128], replicated, may hold values from 0 to 63, as said below
- box_lengths: int32 [8], replicated, may hold values from 1 to 64, as said below
Outputs:
- dedispersed: float32 [256, 64, 256], P(('groups', 'freq')), parts along dimension 0
- box_scores: float32 [256, 8, 64], P(('groups', 'freq')), parts along dimension 0
- peak_per_beam: float32 [128], P('groups'), parts along dimension 0
The draws below stay inside these ranges and needn't reach their ends.
There are 2 independent parts, one for each index of `groups`. The reference program is written for one: setup_inputs(seed, part) draws one part's arguments, and reference() takes and returns one part's arrays. A program takes and returns all parts, laid end to end along the dimension named above; an argument that names none is the same for every part. Nothing has to cross between parts.
Inputs may be any that keep to these rules, and one draw needn't show every extreme that they name: `fdmt_offsets`: at level k every entry is below 4 * 2^k. Within each merged subband both rows are nondecreasing in d and rise by at most one per step; their sum is d except where the upper row stops at its largest value. `box_lengths`: the last filter is exactly 64 samples long.
All inputs are finite; a program needn't handle non-finite values.
Results may differ from the reference program's by a relative error of at most 0.0024.
The reference program's roundings to bfloat16 on the way count: a program that leaves them out, or rounds other values in their place, can miss the bound.
Values sent between devices are 32-bit elements; how exact they have to be, the bound alone decides.
No kernel may reach another device: no remote copies, remote signals or barrier semaphores. Data moves between devices by JAX's collectives and lax.ppermute only.
A program may use at most 64 MiB of HBM per device.

```python
import math
import jax
import jax.numpy as jnp
from jax import lax

ANTENNA_COUNT = 2048
BEAM_COUNT = 64
S = 256
TAPS = 8
POLYPHASE_COUNT = 2
RATE = 4
NBOX = 8
WMAX = 64
COARSE_CHANNELS = 16
FINE_CHANNELS = 32
DELAYS = 128
LEVELS = 5
BRANCH_SAMPLES = 263
ROWS = 128


def draw_voltages(key, part):
    noise_key, sample_time_key, antenna_key = jax.random.split(key, 3)
    complete_shape = (COARSE_CHANNELS, BRANCH_SAMPLES, POLYPHASE_COUNT, 2, ANTENNA_COUNT)
    noise_component = jax.random.normal(noise_key, complete_shape, jnp.float32)
    temporal_gain = jnp.exp(jax.random.uniform(sample_time_key, (COARSE_CHANNELS, BRANCH_SAMPLES, 1, 1, 1), jnp.float32, -1.0, 1.0))
    antenna_gain = jnp.exp(jax.random.uniform(antenna_key, (1, 1, 1, 1, ANTENNA_COUNT), jnp.float32, -0.7, 0.7))
    value_array = noise_component * temporal_gain * antenna_gain
    return jnp.clip(value_array, -12.0, 12.0).astype(jnp.bfloat16)


def draw_fdmt_offsets(key, part):
    tables = []
    for level_index in range(LEVELS):
        child_rows = RATE * 2 ** level_index
        out_rows = 2 * child_rows
        band_count = DELAYS // out_rows
        fraction = jax.random.randint(jax.random.fold_in(key, level_index + 11), (band_count, 1), 16, 48)
        delay_index = jnp.arange(out_rows, dtype=jnp.int32)[None, :]
        low_rows = jnp.minimum(jnp.maximum(delay_index * fraction // 64, delay_index - child_rows + 1), child_rows - 1)
        high_rows = jnp.minimum(delay_index - low_rows, child_rows - 1)
        tables.append(jnp.stack([low_rows.reshape(-1), high_rows.reshape(-1)], 0))
    return jnp.stack(tables, 0).astype(jnp.int32)


def draw_box_lengths(key, part):
    shorter = jax.random.randint(jax.random.fold_in(key, 5), (NBOX - 1,), 1, WMAX)
    return jnp.concatenate([shorter, jnp.full((1,), WMAX, jnp.int32)]).astype(jnp.int32)


def block_levels(own_key, shape, cuts, low, high):
    gain = 1.0
    for dim, blocks in cuts:
        heights = jax.random.uniform(jax.random.fold_in(jax.random.fold_in(own_key, 6), dim), (blocks,), jnp.float32, low / len(cuts), high / len(cuts))
        gain = gain * jnp.repeat(jnp.exp(heights), shape[dim] // blocks).reshape((-1,) + (1,) * (len(shape) - 1 - dim))
    return gain


def gaussian(key, extent, width, reach, cuts=(), kind=jnp.bfloat16):
    drawn = width * jax.random.normal(key, extent, jnp.float32)
    if cuts:
        drawn = drawn * block_levels(key, extent, cuts, -0.22, 0.18)
    return jnp.clip(drawn, -reach, reach).astype(kind)


def setup_inputs(seed: int = 0, part: int = 0) -> dict:
    keys = jax.random.split(jax.random.key(seed), 6)
    part_keys = jax.random.split(jax.random.fold_in(keys[5], part), 6)
    return {
        "voltages": draw_voltages(jax.random.fold_in(jax.random.fold_in(keys[5], part), 71), part),
        "pfb_taps": jnp.clip(jax.random.uniform(keys[1], (TAPS, POLYPHASE_COUNT), jnp.float32, 0.2, 1.0), 0.2, 1.0),
        "steering": gaussian(part_keys[2], (FINE_CHANNELS, 2, ANTENNA_COUNT, BEAM_COUNT), (2 * ANTENNA_COUNT) ** -0.5, 0.09375, ((0, 16),)),
        "fdmt_offsets": draw_fdmt_offsets(jax.random.fold_in(keys[5], 71), part),
        "box_lengths": draw_box_lengths(jax.random.fold_in(keys[5], 71), part),
    }


def shift_time(value_array, amount):
    length = value_array.shape[-1]
    if amount >= length:
        return jnp.zeros_like(value_array)
    zeros_part = jnp.zeros(value_array.shape[:-1] + (amount,), value_array.dtype)
    return jnp.concatenate([zeros_part, value_array[..., :length - amount]], axis=-1)

def delay_rows(value_array, lag_rows, child_rows):
    result = value_array
    for section_bit in range(max(child_rows - 1, 0).bit_length()):
        step_size = 1 << section_bit
        chosen = lag_rows >> section_bit & 1 == 1
        result = jnp.where(chosen[:, :, None, None], shift_time(result, step_size), result)
    return result

def take_band(band_rows, row_index):
    return jnp.take(band_rows, row_index, axis=0)

def merge_bands(lower_band, upper_band, low_rows, high_rows):
    child_rows = lower_band.shape[1]
    from_lower = jax.vmap(take_band)(lower_band, low_rows)
    from_upper = delay_rows(jax.vmap(take_band)(upper_band, high_rows), low_rows, child_rows)
    return from_lower + from_upper

def first_plane(cleaned, delay_rate):
    running_sum = cleaned
    term_list = [cleaned]
    for lag_count in range(1, delay_rate):
        running_sum = running_sum + shift_time(cleaned, lag_count)
        term_list.append(running_sum)
    return jnp.stack(term_list, 1)

def normalize(power_rows):
    level_mean = lax.optimization_barrier(jnp.mean(power_rows, axis=-1, keepdims=True))
    centered = power_rows - level_mean
    spread = lax.optimization_barrier(jnp.mean(centered * centered, axis=-1, keepdims=True))
    return centered / jnp.sqrt(spread + 1e-05)

def reference(voltages, pfb_taps, steering, fdmt_offsets, box_lengths):

    def single_coarse(pieces):
        volume, weight_pair = pieces
        samples = S
        filtered = pfb_taps[0][None, :, None, None] * volume[0:samples].astype(jnp.float32)
        for tap_index in range(1, TAPS):
            filtered = filtered + pfb_taps[tap_index][None, :, None, None] * volume[tap_index:tap_index + samples].astype(jnp.float32)
        fine_sum = (filtered[:, 0] + filtered[:, 1]).astype(jnp.bfloat16)
        fine_diff = (filtered[:, 0] - filtered[:, 1]).astype(jnp.bfloat16)
        powers = []
        for channel, fine_data in enumerate((fine_sum, fine_diff)):
            weights = weight_pair[channel]
            stacked = jnp.concatenate([jnp.concatenate([weights[0], weights[1]], 1), jnp.concatenate([-weights[1], weights[0]], 1)], 0)
            beam_out = jnp.dot(fine_data.reshape(samples, -1), stacked, preferred_element_type=jnp.float32)
            real_part = beam_out[:, :BEAM_COUNT]
            imag_part = beam_out[:, BEAM_COUNT:]
            powers.append((real_part * real_part + imag_part * imag_part).T)
        return jnp.stack(powers, 0)
    every_power = lax.map(single_coarse, (voltages, steering.reshape(COARSE_CHANNELS, POLYPHASE_COUNT, 2, ANTENNA_COUNT, BEAM_COUNT)))
    every_power = every_power.reshape(FINE_CHANNELS, BEAM_COUNT, S)
    normed = normalize(every_power)
    cleaned = normed - lax.optimization_barrier(jnp.mean(normed, axis=0, keepdims=True))
    plane_now = first_plane(cleaned, RATE)
    for level_index in range(LEVELS):
        band_count = plane_now.shape[0]
        child_rows = plane_now.shape[1]
        paired = plane_now.reshape(band_count // 2, 2, child_rows, BEAM_COUNT, S)
        low_rows = fdmt_offsets[level_index, 0].reshape(band_count // 2, 2 * child_rows)
        high_rows = fdmt_offsets[level_index, 1].reshape(band_count // 2, 2 * child_rows)
        plane_now = merge_bands(paired[:, 0], paired[:, 1], low_rows, high_rows)
    full_plane = plane_now[0] / math.sqrt(FINE_CHANNELS)
    dedispersed = jnp.transpose(full_plane.reshape(2, DELAYS // 2, BEAM_COUNT, S), (0, 2, 1, 3)).reshape(ROWS, DELAYS // 2, S)
    running = jnp.cumsum(dedispersed, axis=-1)
    padded = jnp.concatenate([jnp.zeros(running.shape[:-1] + (S,), jnp.float32), running], -1)
    score_list = []
    for box_index in range(NBOX):
        box_width = box_lengths[box_index]
        lagged = lax.dynamic_slice_in_dim(padded, (S - box_width).astype(jnp.int32), S, axis=2)
        score_list.append(lax.optimization_barrier(jnp.max((running - lagged) / jnp.sqrt(box_width.astype(jnp.float32)), axis=-1)))
    box_scores = jnp.stack(score_list, 1)
    peak_per_beam = lax.optimization_barrier(jnp.max(box_scores.reshape(2, BEAM_COUNT, NBOX, DELAYS // 2), axis=(0, 2, 3)))
    return (dedispersed, box_scores, peak_per_beam)
```

```python
import math

import jax
import jax.numpy as jnp
from jax import lax
from jax.sharding import PartitionSpec as P


def shift_time(value_array, amount):
    length = value_array.shape[-1]
    if amount >= length:
        return jnp.zeros_like(value_array)
    zeros_part = jnp.zeros(value_array.shape[:-1] + (amount,), value_array.dtype)
    return jnp.concatenate([zeros_part, value_array[..., : length - amount]], axis=-1)


def delay_rows(value_array, lag_rows, child_rows):
    result = value_array
    for section_bit in range(max(child_rows - 1, 0).bit_length()):
        step_size = 1 << section_bit
        chosen = lag_rows >> section_bit & 1 == 1
        result = jnp.where(chosen[:, :, None, None], shift_time(result, step_size), result)
    return result


def take_band(band_rows, row_index):
    return jnp.take(band_rows, row_index, axis=0)


def merge_bands(lower_band, upper_band, low_rows, high_rows):
    child_rows = lower_band.shape[1]
    from_lower = jax.vmap(take_band)(lower_band, low_rows)
    from_upper = delay_rows(jax.vmap(take_band)(upper_band, high_rows), low_rows, child_rows)
    return from_lower + from_upper


def first_plane(cleaned, delay_rate):
    running_sum = cleaned
    term_list = [cleaned]
    for lag_count in range(1, delay_rate):
        running_sum = running_sum + shift_time(cleaned, lag_count)
        term_list.append(running_sum)
    return jnp.stack(term_list, 1)


def normalize(power_rows):
    level_mean = jnp.mean(power_rows, axis=-1, keepdims=True)
    centered = power_rows - level_mean
    spread = jnp.mean(centered * centered, axis=-1, keepdims=True)
    return centered / jnp.sqrt(spread + 1e-05)


def beam_powers(volume, pfb_taps, weight_pair):
    tap_total = pfb_taps.shape[0]
    samples = volume.shape[0] - tap_total + 1
    beam_total = weight_pair.shape[-1]
    filtered = pfb_taps[0][None, :, None, None] * volume[0:samples].astype(jnp.float32)
    for tap_index in range(1, tap_total):
        filtered = filtered + pfb_taps[tap_index][None, :, None, None] * volume[
            tap_index : tap_index + samples
        ].astype(jnp.float32)
    fine_sum = (filtered[:, 0] + filtered[:, 1]).astype(jnp.bfloat16)
    fine_diff = (filtered[:, 0] - filtered[:, 1]).astype(jnp.bfloat16)
    powers = []
    for channel, fine_data in enumerate((fine_sum, fine_diff)):
        weights = weight_pair[channel]
        stacked = jnp.concatenate(
            [
                jnp.concatenate([weights[0], weights[1]], 1),
                jnp.concatenate([-weights[1], weights[0]], 1),
            ],
            0,
        )
        beam_out = jnp.einsum(
            "kb,sk->bs", stacked, fine_data.reshape(samples, -1), preferred_element_type=jnp.float32
        )
        real_part = beam_out[:beam_total]
        imag_part = beam_out[beam_total:]
        powers.append(real_part * real_part + imag_part * imag_part)
    return jnp.stack(powers, 1)


def shards(voltages, pfb_taps, steering, fdmt_offsets, box_lengths):
    devices = lax.axis_size("freq")
    device_id = lax.axis_index("freq")
    beam_total = steering.shape[-1]
    level_count = fdmt_offsets.shape[0]
    delays = fdmt_offsets.shape[-1]
    channels = 2 * devices
    delay_rate = delays // channels
    top_bit = devices.bit_length() - 2
    per_device = 2 * beam_total // devices
    half_rows = delays // 2
    half_index = device_id >> top_bit
    final_rows = lax.dynamic_slice_in_dim(
        fdmt_offsets[level_count - 1], half_index * half_rows, half_rows, axis=1
    )
    normed = normalize(beam_powers(voltages[0], pfb_taps, steering))
    outgoing = jnp.broadcast_to(normed[None], (2,) + normed.shape).reshape(
        devices, per_device, 2, normed.shape[-1]
    )
    incoming = lax.all_to_all(outgoing, "freq", split_axis=0, concat_axis=0, tiled=True)
    by_channel = jnp.transpose(incoming, (0, 2, 1, 3)).reshape(channels, per_device, -1)
    cleaned = by_channel - jnp.mean(by_channel, axis=0, keepdims=True)
    plane_now = first_plane(cleaned, delay_rate)
    for level_index in range(level_count - 1):
        band_count = plane_now.shape[0]
        child_rows = plane_now.shape[1]
        paired = plane_now.reshape(band_count // 2, 2, child_rows, per_device, plane_now.shape[-1])
        level_rows = fdmt_offsets[level_index].reshape(2, band_count // 2, 2 * child_rows)
        plane_now = merge_bands(paired[:, 0], paired[:, 1], level_rows[0], level_rows[1])
    final_plane = merge_bands(plane_now[0:1], plane_now[1:2], final_rows[0:1], final_rows[1:2])[0]
    scaled = final_plane / math.sqrt(channels)
    dedispersed = jnp.transpose(scaled, (1, 0, 2))
    samples = dedispersed.shape[-1]
    running = jnp.cumsum(dedispersed, axis=-1)
    padded = jnp.concatenate([jnp.zeros(running.shape[:-1] + (samples,), jnp.float32), running], -1)
    score_list = []
    for box_index in range(box_lengths.shape[0]):
        box_width = box_lengths[box_index]
        lagged = lax.dynamic_slice_in_dim(padded, samples - box_width, samples, axis=2)
        score_list.append(
            jnp.max((running - lagged) / jnp.sqrt(box_width.astype(jnp.float32)), axis=-1)
        )
    box_scores = jnp.stack(score_list, 1)
    local_best = jnp.max(box_scores, axis=(1, 2))
    beam_start = device_id % (devices // 2) * per_device
    contrib = lax.dynamic_update_slice(
        jnp.full((beam_total,), -1e30, jnp.float32), local_best, (beam_start,)
    )
    peak_per_beam = contrib
    step = 1
    while step < devices:
        pairs = [(place, place ^ step) for place in range(devices)]
        peak_per_beam = jnp.maximum(peak_per_beam, lax.ppermute(peak_per_beam, "freq", pairs))
        step *= 2
    return (dedispersed, box_scores, peak_per_beam)


def solution(mesh):
    placed = (
        P(("groups", "freq"), None, None, None, None),
        P(),
        P(("groups", "freq"), None, None, None),
        P(),
        P(),
    )
    return jax.shard_map(
        shards,
        mesh=mesh,
        in_specs=placed,
        out_specs=(
            P(("groups", "freq"), None, None),
            P(("groups", "freq"), None, None),
            P("groups"),
        ),
        check_vma=False,
    )
```

```python
import functools
import math

import jax
import jax.numpy as jnp
from jax import lax
from jax.experimental import pallas as pl
from jax.experimental.pallas import tpu as pltpu
from jax.sharding import PartitionSpec as P


def k1_kernel(chunk, taps_ref, x_hbm, w_hbm, out_ref, slab, wbuf, fine, x_sem, w_sem):
    tap_total, branches = taps_ref.shape
    rows_in, tiles = x_hbm.shape[0], x_hbm.shape[1]
    samples = fine.shape[2]
    beams2 = wbuf.shape[1]
    beams = beams2 // 2
    flat = slab.reshape(tiles, 2 * slab.shape[1], 128)
    window = -(-4 * (chunk + tap_total - 1) // 16) * 16

    def x_copy(j):
        return pltpu.make_async_copy(x_hbm.at[:, j], slab.at[j, pl.ds(0, rows_in)], x_sem.at[j])

    for j in range(tiles):
        x_copy(j).start()
    w_copy = pltpu.make_async_copy(w_hbm, wbuf, w_sem)
    w_copy.start()
    shape = (2, 2, chunk, window)
    col = lax.broadcasted_iota(jnp.int32, shape, 3)
    part = lax.broadcasted_iota(jnp.int32, shape, 0)
    fsel = lax.broadcasted_iota(jnp.int32, shape, 1)
    tap = (col >> 2) - lax.broadcasted_iota(jnp.int32, shape, 2)
    branch = (col >> 1) & 1
    code = jnp.where((col & 1) == part, tap * 2 + branch, -1)
    weights = jnp.zeros(shape, jnp.float32)
    for k in range(tap_total):
        for p in range(branches):
            weights = jnp.where(code == 2 * k + p, taps_ref[k, p], weights)
    weights = jnp.where((fsel & branch) == 1, -weights, weights).reshape(4 * chunk, window)
    high = weights.astype(jnp.bfloat16)
    low = (weights - high.astype(jnp.float32)).astype(jnp.bfloat16)
    both = jnp.concatenate([high, low], 0)
    starts = list(range(0, samples - chunk, chunk)) + [samples - chunk]

    def pair(g, carry):
        x_copy(2 * g).wait()
        x_copy(2 * g + 1).wait()
        for s0 in starts:
            pieces = [flat[2 * g + i, pl.ds(4 * s0, window), :] for i in range(2)]
            got = jnp.dot(both, jnp.concatenate(pieces, 1), preferred_element_type=jnp.float32)
            rounded = (got[: 4 * chunk] + got[4 * chunk :]).astype(jnp.bfloat16)
            for q in range(4):
                fine[q // 2, q % 2, pl.ds(s0, chunk), pl.ds(pl.multiple_of(256 * g, 256), 256)] = rounded[q * chunk : (q + 1) * chunk]
        return carry

    for j in range(tiles):
        spare = slab.shape[1] - rows_in
        if spare:
            slab[j, pl.ds(rows_in, spare)] = jnp.zeros((spare, 2, 128), jnp.bfloat16)
    lax.fori_loop(0, tiles // 2, pair, 0)
    w_copy.wait()
    for f in range(2):
        dims = (((1,), (1,)), ((), ()))
        got_re = lax.dot_general(wbuf[f], fine[0, f], dims, preferred_element_type=jnp.float32)
        got_im = lax.dot_general(wbuf[f], fine[1, f], dims, preferred_element_type=jnp.float32)
        beam_re = got_re[:beams] - got_im[beams:]
        beam_im = got_re[beams:] + got_im[:beams]
        power = beam_re * beam_re + beam_im * beam_im
        level = jnp.mean(power, axis=-1, keepdims=True)
        centered = power - level
        spread = jnp.mean(centered * centered, axis=-1, keepdims=True)
        normed = centered / jnp.sqrt(spread + 1e-05)
        if out_ref.ndim == 5:
            normed = normed.reshape(out_ref.shape[1], out_ref.shape[3], samples)
            for h in range(2):
                out_ref[h, :, f] = normed
        else:
            out_ref[f] = normed

def k1(taps, volume, steering, per):
    t, branches, parts, antennas = volume.shape
    tap_total = taps.shape[0]
    samples = t - tap_total + 1
    beams = steering.shape[-1]
    tiles = antennas // 128
    x = volume.reshape(t * 2, 2, tiles, 128).transpose(0, 2, 1, 3)
    w = steering.transpose(0, 1, 3, 2).reshape(2, 2 * beams, antennas)
    chunk = (64 - tap_total + 1) // 16 * 16
    depth = -(-4 * t // 16) * 16
    out_dims = (2, beams // per, 2, per, samples) if per % 8 == 0 else (2, beams, samples)
    return pl.pallas_call(
        functools.partial(k1_kernel, chunk),
        out_shape=jax.ShapeDtypeStruct(out_dims, jnp.float32),
        in_specs=[
            pl.BlockSpec(memory_space=pltpu.SMEM),
            pl.BlockSpec(memory_space=pltpu.HBM),
            pl.BlockSpec(memory_space=pltpu.HBM),
        ],
        out_specs=pl.BlockSpec(memory_space=pltpu.VMEM),
        scratch_shapes=[
            pltpu.VMEM((tiles, depth // 2, 2, 128), jnp.bfloat16),
            pltpu.VMEM((2, 2 * beams, antennas), jnp.bfloat16),
            pltpu.VMEM((2, 2, samples, antennas), jnp.bfloat16),
            pltpu.SemaphoreType.DMA((tiles,)),
            pltpu.SemaphoreType.DMA,
        ],
        compiler_params=pltpu.CompilerParams(vmem_limit_bytes=50 << 20),
        name="channelize",
    )(taps, x, w)


UNROLL = 32

def shift_static(value, amount):
    rolled = pltpu.roll(value, amount, 1)
    lane = lax.broadcasted_iota(jnp.int32, value.shape, 1)
    return jnp.where(lane >= amount, rolled, 0.0)

def shift_dynamic(value, amount, limit):
    tiles = value.shape[-1] // 128
    pieces = [value[:, 128 * t : 128 * t + 128] for t in range(tiles)]
    lane = lax.broadcasted_iota(jnp.int32, pieces[0].shape, 1)
    zero = jnp.zeros_like(pieces[0])
    rest = amount
    if limit > 128:
        whole = amount >> 7
        rest = amount & 127
        moved = list(pieces)
        for t in range(tiles):
            moved[t] = zero
            for q in range(t + 1):
                moved[t] = jnp.where(whole == q, pieces[t - q], moved[t])
        pieces = moved
    rolled = [pltpu.roll(piece, rest, 1) for piece in pieces]
    kept = lane >= rest
    out = [jnp.where(kept, rolled[t], rolled[t - 1] if t else zero) for t in range(tiles)]
    return jnp.concatenate(out, 1)

def k2_kernel(place_ref, offsets_ref, boxes_ref, normed_ref, dedispersed_ref, scores_ref, peak_ref, planes, other, ramp):
    channels, per, samples = normed_ref.shape
    level_total = offsets_ref.shape[0]
    delays = planes.shape[1]
    rate = delays // channels
    half_rows = delays // 2
    half = place_ref[0]
    block = place_ref[1]
    total = normed_ref[0]
    for c in range(1, channels):
        total = total + normed_ref[c]
    common = total * (1.0 / channels)

    def first(i, carry):
        terms = []
        for u in range(4):
            cleaned = normed_ref[4 * i + u] - common
            terms.append(cleaned)
            for lag in range(1, rate):
                terms.append(terms[-1] + shift_static(cleaned, lag))
        for u in range(4 * rate):
            planes[0, 4 * rate * i + u] = terms[u]
        return carry

    lax.fori_loop(0, channels // 4, first, 0)

    def merged(level, row):
        out_rows = rate << (level + 1)
        child = out_rows // 2
        low = offsets_ref[level, 0, row]
        high = offsets_ref[level, 1, row]
        base = row & ~(out_rows - 1)
        upper = planes[level % 2, base + child + high]
        return planes[level % 2, base + low] + shift_dynamic(upper, low, child)

    for level in range(level_total - 1):
        def one(i, carry, level=level):
            rows = [merged(level, UNROLL * i + u) for u in range(UNROLL)]
            for u in range(UNROLL):
                planes[(level + 1) % 2, UNROLL * i + u] = rows[u]
            return carry
        lax.fori_loop(0, delays // UNROLL, one, 0)

    scale = 1.0 / math.sqrt(channels)
    level = level_total - 1
    for own in range(2):
        start = (half if own == 0 else 1 - half) * half_rows
        target = dedispersed_ref if own == 0 else other
        def last(i, carry, start=start, target=target):
            rows = [merged(level, start + UNROLL * i + u) * scale for u in range(UNROLL)]
            if per % 8 == 0:
                target[:, pl.ds(pl.multiple_of(UNROLL * i, UNROLL), UNROLL), :] = jnp.transpose(jnp.stack(rows, 0), (1, 0, 2))
            else:
                for u in range(UNROLL):
                    for b in range(per):
                        target[b, pl.ds(UNROLL * i + u, 1), :] = rows[u][b : b + 1]
            return carry
        lax.fori_loop(0, half_rows // UNROLL, last, 0)

    width = per * half_rows
    later = lax.broadcasted_iota(jnp.int32, (samples, samples), 0)
    earlier = lax.broadcasted_iota(jnp.int32, (samples, samples), 1)
    upto = jnp.where(earlier <= later, 1.0, 0.0).astype(jnp.bfloat16)
    groups = width // 128
    for g in range(groups):
        ramp[g, pl.ds(0, samples), :] = jnp.zeros((samples, 128), jnp.float32)
    best = None
    for own in range(2):
        source = dedispersed_ref if own == 0 else other
        rest = source[...].reshape(width, samples)
        running = None
        for piece in range(3):
            part = rest.astype(jnp.bfloat16)
            if piece < 2:
                rest = rest - part.astype(jnp.float32)
            got = lax.dot_general(upto, part, (((1,), (1,)), ((), ())), preferred_element_type=jnp.float32)
            running = got if running is None else running + got
        for g in range(groups):
            ramp[g, pl.ds(samples, samples), :] = running[:, 128 * g : 128 * g + 128]
        found = []
        for w in range(boxes_ref.shape[0]):
            length = boxes_ref[w]
            root = jnp.sqrt(jnp.full((1, 128), length, jnp.int32).astype(jnp.float32))
            peaks_here = []
            for g in range(groups):
                response = ramp[g, pl.ds(samples, samples), :] - ramp[g, pl.ds(samples - length, samples), :]
                peaks_here.append(jnp.max(response, axis=0, keepdims=True) / root)
            found.append(jnp.concatenate(peaks_here, 1))
        table = jnp.concatenate(found, 0)
        if own == 0:
            for b in range(per):
                scores_ref[b] = table[:, half_rows * b : half_rows * (b + 1)]
        top = jnp.max(table, axis=0, keepdims=True)
        best = top if best is None else jnp.maximum(best, top)
    lane = lax.broadcasted_iota(jnp.int32, peak_ref.shape, 1)
    peaks = jnp.full(peak_ref.shape, -jnp.inf, jnp.float32)
    for b in range(per):
        one_beam = jnp.max(best[:, half_rows * b : half_rows * (b + 1)], axis=1, keepdims=True)
        peaks = jnp.where(lane == block * per + b, one_beam, peaks)
    peak_ref[...] = peaks

def k2(place, offsets, boxes, normed, beams):
    channels, per, samples = normed.shape
    delays = offsets.shape[-1]
    half_rows = delays // 2
    smem = pl.BlockSpec(memory_space=pltpu.SMEM)
    vmem = pl.BlockSpec(memory_space=pltpu.VMEM)
    return pl.pallas_call(
        k2_kernel,
        out_shape=(
            jax.ShapeDtypeStruct((per, half_rows, samples), jnp.float32),
            jax.ShapeDtypeStruct((per, boxes.shape[0], half_rows), jnp.float32),
            jax.ShapeDtypeStruct((1, beams), jnp.float32),
        ),
        in_specs=[smem, smem, smem, vmem],
        out_specs=(vmem, vmem, vmem),
        scratch_shapes=[
            pltpu.VMEM((2, delays, per, samples), jnp.float32),
            pltpu.VMEM((per, half_rows, samples), jnp.float32),
            pltpu.VMEM((per * half_rows // 128, 2 * samples, 128), jnp.float32),
        ],
        compiler_params=pltpu.CompilerParams(vmem_limit_bytes=50 << 20),
        name="dedisperse",
    )(place, offsets, boxes, normed)


def shards(voltages, pfb_taps, steering, fdmt_offsets, box_lengths):
    devices = lax.axis_size("freq")
    device_id = lax.axis_index("freq")
    beams = steering.shape[-1]
    blocks = devices // 2
    per = beams // blocks
    samples = voltages.shape[1] - pfb_taps.shape[0] + 1
    normed = k1(pfb_taps, voltages[0], steering, per)
    if normed.ndim == 3:
        normed = normed.reshape(2, blocks, per, samples).transpose(1, 0, 2, 3)
        normed = jnp.broadcast_to(normed[None], (2,) + normed.shape)
    outgoing = normed.reshape(devices, 2, per, samples)
    incoming = lax.all_to_all(outgoing, "freq", split_axis=0, concat_axis=0, tiled=True)
    place = jnp.stack([device_id // blocks, device_id % blocks]).astype(jnp.int32)
    dedispersed, box_scores, peaks = k2(
        place, fdmt_offsets, box_lengths, incoming.reshape(2 * devices, per, samples), beams
    )
    step = 1
    while step < blocks:
        pairs = [(spot, spot ^ step) for spot in range(devices)]
        peaks = jnp.maximum(peaks, lax.ppermute(peaks, "freq", pairs))
        step *= 2
    return (dedispersed, box_scores, peaks.reshape(beams))


def solution(mesh):
    placed = (
        P(("groups", "freq"), None, None, None, None),
        P(),
        P(("groups", "freq"), None, None, None),
        P(),
        P(),
    )
    return jax.shard_map(
        shards,
        mesh=mesh,
        in_specs=placed,
        out_specs=(
            P(("groups", "freq"), None, None),
            P(("groups", "freq"), None, None),
            P("groups"),
        ),
        check_vma=False,
    )
```

```python
import functools
import math

import jax
import jax.numpy as jnp
from jax import lax
from jax.experimental import pallas as pl
from jax.experimental.pallas import tpu as pltpu
from jax.sharding import PartitionSpec as P


def k1_kernel(chunk, taps_hbm, x_hbm, w_hbm, out_ref, slab, wbuf, fine, taps_ref, x_sem, w_sem, taps_sem):
    branches, tap_total = taps_ref.shape
    rows_in, tiles = x_hbm.shape[0], x_hbm.shape[1]
    samples = fine.shape[2]
    beams2 = wbuf.shape[1]
    beams = beams2 // 2
    flat = slab.reshape(tiles, 2 * slab.shape[1], 128)
    window = -(-4 * (chunk + tap_total - 1) // 16) * 16

    def x_copy(j):
        return pltpu.make_async_copy(x_hbm.at[:, j], slab.at[j, pl.ds(0, rows_in)], x_sem.at[j])

    taps_copy = pltpu.make_async_copy(taps_hbm, taps_ref, taps_sem)
    taps_copy.start()
    for j in range(tiles):
        x_copy(j).start()
    w_copy = pltpu.make_async_copy(w_hbm, wbuf, w_sem)
    w_copy.start()
    taps_copy.wait()
    shape = (2, 2, chunk, window)
    col = lax.broadcasted_iota(jnp.int32, shape, 3)
    part = lax.broadcasted_iota(jnp.int32, shape, 0)
    fsel = lax.broadcasted_iota(jnp.int32, shape, 1)
    tap = (col >> 2) - lax.broadcasted_iota(jnp.int32, shape, 2)
    branch = (col >> 1) & 1
    code = jnp.where((col & 1) == part, tap * 2 + branch, -1)
    weights = jnp.zeros(shape, jnp.float32)
    for k in range(tap_total):
        for p in range(branches):
            weights = jnp.where(code == 2 * k + p, taps_ref[p, k], weights)
    weights = jnp.where((fsel & branch) == 1, -weights, weights).reshape(4 * chunk, window)
    high = weights.astype(jnp.bfloat16)
    low = (weights - high.astype(jnp.float32)).astype(jnp.bfloat16)
    both = jnp.concatenate([high, low], 0)
    starts = list(range(0, samples - chunk, chunk)) + [samples - chunk]

    def pair(g, carry):
        x_copy(2 * g).wait()
        x_copy(2 * g + 1).wait()
        for s0 in starts:
            pieces = [flat[2 * g + i, pl.ds(4 * s0, window), :] for i in range(2)]
            got = jnp.dot(both, jnp.concatenate(pieces, 1), preferred_element_type=jnp.float32)
            rounded = (got[: 4 * chunk] + got[4 * chunk :]).astype(jnp.bfloat16)
            for q in range(4):
                fine[q // 2, q % 2, pl.ds(s0, chunk), pl.ds(pl.multiple_of(256 * g, 256), 256)] = rounded[q * chunk : (q + 1) * chunk]
        return carry

    for j in range(tiles):
        spare = slab.shape[1] - rows_in
        if spare:
            slab[j, pl.ds(rows_in, spare)] = jnp.zeros((spare, 2, 128), jnp.bfloat16)
    lax.fori_loop(0, tiles // 2, pair, 0)
    w_copy.wait()
    for f in range(2):
        dims = (((1,), (1,)), ((), ()))
        got_re = lax.dot_general(wbuf[f], fine[0, f], dims, preferred_element_type=jnp.float32)
        got_im = lax.dot_general(wbuf[f], fine[1, f], dims, preferred_element_type=jnp.float32)
        beam_re = got_re[:beams] - got_im[beams:]
        beam_im = got_re[beams:] + got_im[:beams]
        power = beam_re * beam_re + beam_im * beam_im
        level = jnp.mean(power, axis=-1, keepdims=True)
        centered = power - level
        spread = jnp.mean(centered * centered, axis=-1, keepdims=True)
        normed = centered / jnp.sqrt(spread + 1e-05)
        if out_ref.ndim == 5:
            normed = normed.reshape(out_ref.shape[1], out_ref.shape[3], samples)
            for h in range(2):
                out_ref[h, :, f] = normed
        else:
            out_ref[f] = normed

def k1(taps, volume, steering, per):
    t, branches, parts, antennas = volume.shape
    tap_total = taps.shape[0]
    samples = t - tap_total + 1
    beams = steering.shape[-1]
    tiles = antennas // 128
    x = volume.reshape(t * 2, 2, tiles, 128).transpose(0, 2, 1, 3)
    w = steering.transpose(0, 1, 3, 2).reshape(2, 2 * beams, antennas)
    chunk = (64 - tap_total + 1) // 16 * 16
    depth = -(-4 * t // 16) * 16
    out_dims = (2, beams // per, 2, per, samples) if per % 8 == 0 else (2, beams, samples)
    return pl.pallas_call(
        functools.partial(k1_kernel, chunk),
        out_shape=jax.ShapeDtypeStruct(out_dims, jnp.float32),
        in_specs=[pl.BlockSpec(memory_space=pltpu.HBM)] * 3,
        out_specs=pl.BlockSpec(memory_space=pltpu.VMEM),
        scratch_shapes=[
            pltpu.VMEM((tiles, depth // 2, 2, 128), jnp.bfloat16),
            pltpu.VMEM((2, 2 * beams, antennas), jnp.bfloat16),
            pltpu.VMEM((2, 2, samples, antennas), jnp.bfloat16),
            pltpu.SMEM((2, tap_total), jnp.float32),
            pltpu.SemaphoreType.DMA((tiles,)),
            pltpu.SemaphoreType.DMA,
            pltpu.SemaphoreType.DMA,
        ],
        compiler_params=pltpu.CompilerParams(vmem_limit_bytes=67043328),
        name="channelize",
    )(taps.T, x, w)


UNROLL = 32

def shift_static(value, amount):
    rolled = pltpu.roll(value, amount, 1)
    lane = lax.broadcasted_iota(jnp.int32, value.shape, 1)
    return jnp.where(lane >= amount, rolled, 0.0)

def shift_dynamic(value, amount, limit):
    tiles = value.shape[-1] // 128
    pieces = [value[:, 128 * t : 128 * t + 128] for t in range(tiles)]
    lane = lax.broadcasted_iota(jnp.int32, pieces[0].shape, 1)
    zero = jnp.zeros_like(pieces[0])
    rest = amount
    if limit > 128:
        whole = amount >> 7
        rest = amount & 127
        moved = list(pieces)
        for t in range(tiles):
            moved[t] = zero
            for q in range(t + 1):
                moved[t] = jnp.where(whole == q, pieces[t - q], moved[t])
        pieces = moved
    rolled = [pltpu.roll(piece, rest, 1) for piece in pieces]
    kept = lane >= rest
    out = [jnp.where(kept, rolled[t], rolled[t - 1] if t else zero) for t in range(tiles)]
    return jnp.concatenate(out, 1)

def k2_kernel(place_ref, offsets_ref, boxes_ref, normed_ref, dedispersed_ref, scores_ref, peak_ref, planes, other, ramp):
    channels, per, samples = normed_ref.shape
    level_total = offsets_ref.shape[0]
    delays = planes.shape[1]
    rate = delays // channels
    half_rows = delays // 2
    half = place_ref[0]
    block = place_ref[1]
    total = normed_ref[0]
    for c in range(1, channels):
        total = total + normed_ref[c]
    common = total * (1.0 / channels)

    def first(i, carry):
        terms = []
        for u in range(4):
            cleaned = normed_ref[4 * i + u] - common
            terms.append(cleaned)
            for lag in range(1, rate):
                terms.append(terms[-1] + shift_static(cleaned, lag))
        for u in range(4 * rate):
            planes[0, 4 * rate * i + u] = terms[u]
        return carry

    lax.fori_loop(0, channels // 4, first, 0)

    def merged(level, row):
        out_rows = rate << (level + 1)
        child = out_rows // 2
        low = offsets_ref[level, 0, row]
        high = offsets_ref[level, 1, row]
        base = row & ~(out_rows - 1)
        upper = planes[level % 2, base + child + high]
        return planes[level % 2, base + low] + shift_dynamic(upper, low, child)

    for level in range(level_total - 1):
        def one(i, carry, level=level):
            rows = [merged(level, UNROLL * i + u) for u in range(UNROLL)]
            for u in range(UNROLL):
                planes[(level + 1) % 2, UNROLL * i + u] = rows[u]
            return carry
        lax.fori_loop(0, delays // UNROLL, one, 0)

    scale = 1.0 / math.sqrt(channels)
    level = level_total - 1
    for own in range(2):
        start = (half if own == 0 else 1 - half) * half_rows
        target = dedispersed_ref if own == 0 else other
        def last(i, carry, start=start, target=target):
            rows = [merged(level, start + UNROLL * i + u) * scale for u in range(UNROLL)]
            if per % 8 == 0:
                target[:, pl.ds(pl.multiple_of(UNROLL * i, UNROLL), UNROLL), :] = jnp.transpose(jnp.stack(rows, 0), (1, 0, 2))
            else:
                for u in range(UNROLL):
                    for b in range(per):
                        target[b, pl.ds(UNROLL * i + u, 1), :] = rows[u][b : b + 1]
            return carry
        lax.fori_loop(0, half_rows // UNROLL, last, 0)

    width = per * half_rows
    later = lax.broadcasted_iota(jnp.int32, (samples, samples), 0)
    earlier = lax.broadcasted_iota(jnp.int32, (samples, samples), 1)
    upto = jnp.where(earlier <= later, 1.0, 0.0).astype(jnp.bfloat16)
    groups = width // 128
    for g in range(groups):
        ramp[g, pl.ds(0, samples), :] = jnp.zeros((samples, 128), jnp.float32)
    best = None
    for own in range(2):
        source = dedispersed_ref if own == 0 else other
        rest = source[...].reshape(width, samples)
        running = None
        for piece in range(3):
            part = rest.astype(jnp.bfloat16)
            if piece < 2:
                rest = rest - part.astype(jnp.float32)
            got = lax.dot_general(upto, part, (((1,), (1,)), ((), ())), preferred_element_type=jnp.float32)
            running = got if running is None else running + got
        for g in range(groups):
            ramp[g, pl.ds(samples, samples), :] = running[:, 128 * g : 128 * g + 128]
        found = []
        for w in range(boxes_ref.shape[0]):
            length = boxes_ref[w]
            root = jnp.sqrt(jnp.full((1, 128), length, jnp.int32).astype(jnp.float32))
            peaks_here = []
            for g in range(groups):
                response = ramp[g, pl.ds(samples, samples), :] - ramp[g, pl.ds(samples - length, samples), :]
                peaks_here.append(jnp.max(response, axis=0, keepdims=True) / root)
            found.append(jnp.concatenate(peaks_here, 1))
        table = jnp.concatenate(found, 0)
        if own == 0:
            for b in range(per):
                scores_ref[b] = table[:, half_rows * b : half_rows * (b + 1)]
        top = jnp.max(table, axis=0, keepdims=True)
        best = top if best is None else jnp.maximum(best, top)
    lane = lax.broadcasted_iota(jnp.int32, peak_ref.shape, 1)
    peaks = jnp.full(peak_ref.shape, -jnp.inf, jnp.float32)
    for b in range(per):
        one_beam = jnp.max(best[:, half_rows * b : half_rows * (b + 1)], axis=1, keepdims=True)
        peaks = jnp.where(lane == block * per + b, one_beam, peaks)
    peak_ref[...] = peaks

def k2(place, offsets, boxes, normed, beams):
    channels, per, samples = normed.shape
    delays = offsets.shape[-1]
    half_rows = delays // 2
    smem = pl.BlockSpec(memory_space=pltpu.SMEM)
    vmem = pl.BlockSpec(memory_space=pltpu.VMEM)
    return pl.pallas_call(
        k2_kernel,
        out_shape=(
            jax.ShapeDtypeStruct((per, half_rows, samples), jnp.float32),
            jax.ShapeDtypeStruct((per, boxes.shape[0], half_rows), jnp.float32),
            jax.ShapeDtypeStruct((1, beams), jnp.float32),
        ),
        in_specs=[smem, smem, smem, vmem],
        out_specs=(vmem, vmem, vmem),
        scratch_shapes=[
            pltpu.VMEM((2, delays, per, samples), jnp.float32),
            pltpu.VMEM((per, half_rows, samples), jnp.float32),
            pltpu.VMEM((per * half_rows // 128, 2 * samples, 128), jnp.float32),
        ],
        compiler_params=pltpu.CompilerParams(vmem_limit_bytes=50 << 20),
        name="dedisperse",
    )(place, offsets, boxes, normed)


def shards(voltages, pfb_taps, steering, fdmt_offsets, box_lengths):
    devices = lax.axis_size("freq")
    device_id = lax.axis_index("freq")
    beams = steering.shape[-1]
    blocks = devices // 2
    per = beams // blocks
    samples = voltages.shape[1] - pfb_taps.shape[0] + 1
    normed = k1(pfb_taps, voltages[0], steering, per)
    if normed.ndim == 3:
        normed = normed.reshape(2, blocks, per, samples).transpose(1, 0, 2, 3)
        normed = jnp.broadcast_to(normed[None], (2,) + normed.shape)
    outgoing = normed.reshape(devices, 2, per, samples)
    incoming = lax.all_to_all(outgoing, "freq", split_axis=0, concat_axis=0, tiled=True)
    place = jnp.stack([device_id // blocks, device_id % blocks]).astype(jnp.int32)
    dedispersed, box_scores, peaks = k2(
        place, fdmt_offsets, box_lengths, incoming.reshape(2 * devices, per, samples), beams
    )
    step = 1
    while step < blocks:
        pairs = [(spot, spot ^ step) for spot in range(devices)]
        peaks = jnp.maximum(peaks, lax.ppermute(peaks, "freq", pairs))
        step *= 2
    return (dedispersed, box_scores, peaks.reshape(beams))


def solution(mesh):
    placed = (
        P(("groups", "freq"), None, None, None, None),
        P(),
        P(("groups", "freq"), None, None, None),
        P(),
        P(),
    )
    return jax.shard_map(
        shards,
        mesh=mesh,
        in_specs=placed,
        out_specs=(
            P(("groups", "freq"), None, None),
            P(("groups", "freq"), None, None),
            P("groups"),
        ),
        check_vma=False,
    )
```

```python
import functools
import math

import jax
import jax.numpy as jnp
from jax import lax
from jax.experimental import pallas as pl
from jax.experimental.pallas import tpu as pltpu
from jax.sharding import PartitionSpec as P


def k1_kernel(chunk, taps_hbm, x_hbm, w_hbm, out_ref, slab, wbuf, fine, taps_ref, x_sem, w_sem, taps_sem):
    branches, tap_total = taps_ref.shape
    rows_in, tiles = x_hbm.shape[0], x_hbm.shape[1]
    samples = fine.shape[2]
    beams2 = wbuf.shape[1]
    beams = beams2 // 2
    flat = slab.reshape(tiles, 2 * slab.shape[1], 128)
    window = -(-4 * (chunk + tap_total - 1) // 16) * 16

    def x_copy(j):
        return pltpu.make_async_copy(x_hbm.at[:, j], slab.at[j, pl.ds(0, rows_in)], x_sem.at[j])

    taps_copy = pltpu.make_async_copy(taps_hbm, taps_ref, taps_sem)
    taps_copy.start()
    for j in range(tiles):
        x_copy(j).start()
    w_copy = pltpu.make_async_copy(w_hbm, wbuf, w_sem)
    w_copy.start()
    taps_copy.wait()
    shape = (2, 2, chunk, window)
    col = lax.broadcasted_iota(jnp.int32, shape, 3)
    part = lax.broadcasted_iota(jnp.int32, shape, 0)
    fsel = lax.broadcasted_iota(jnp.int32, shape, 1)
    tap = (col >> 2) - lax.broadcasted_iota(jnp.int32, shape, 2)
    branch = (col >> 1) & 1
    code = jnp.where((col & 1) == part, tap * 2 + branch, -1)
    weights = jnp.zeros(shape, jnp.float32)
    for k in range(tap_total):
        for p in range(branches):
            weights = jnp.where(code == 2 * k + p, taps_ref[p, k], weights)
    weights = jnp.where((fsel & branch) == 1, -weights, weights).reshape(4 * chunk, window)
    high = weights.astype(jnp.bfloat16)
    low = (weights - high.astype(jnp.float32)).astype(jnp.bfloat16)
    both = jnp.concatenate([high, low], 0)
    starts = list(range(0, samples - chunk, chunk)) + [samples - chunk]

    def pair(g, carry):
        x_copy(2 * g).wait()
        x_copy(2 * g + 1).wait()
        for s0 in starts:
            pieces = [flat[2 * g + i, pl.ds(4 * s0, window), :] for i in range(2)]
            got = jnp.dot(both, jnp.concatenate(pieces, 1), preferred_element_type=jnp.float32)
            rounded = (got[: 4 * chunk] + got[4 * chunk :]).astype(jnp.bfloat16)
            for q in range(4):
                fine[q // 2, q % 2, pl.ds(s0, chunk), pl.ds(pl.multiple_of(256 * g, 256), 256)] = rounded[q * chunk : (q + 1) * chunk]
        return carry

    for j in range(tiles):
        spare = slab.shape[1] - rows_in
        if spare:
            slab[j, pl.ds(rows_in, spare)] = jnp.zeros((spare, 2, 128), jnp.bfloat16)
    lax.fori_loop(0, tiles // 2, pair, 0)
    w_copy.wait()
    for f in range(2):
        dims = (((1,), (1,)), ((), ()))
        got_re = lax.dot_general(wbuf[f], fine[0, f], dims, preferred_element_type=jnp.float32)
        got_im = lax.dot_general(wbuf[f], fine[1, f], dims, preferred_element_type=jnp.float32)
        beam_re = got_re[:beams] - got_im[beams:]
        beam_im = got_re[beams:] + got_im[:beams]
        power = beam_re * beam_re + beam_im * beam_im
        level = jnp.mean(power, axis=-1, keepdims=True)
        centered = power - level
        spread = jnp.mean(centered * centered, axis=-1, keepdims=True)
        normed = centered / jnp.sqrt(spread + 1e-05)
        if out_ref.ndim == 5:
            normed = normed.reshape(out_ref.shape[1], out_ref.shape[3], samples)
            for h in range(2):
                out_ref[h, :, f] = normed
        else:
            out_ref[f] = normed

def k1(taps, volume, steering, per):
    t, branches, parts, antennas = volume.shape
    tap_total = taps.shape[0]
    samples = t - tap_total + 1
    beams = steering.shape[-1]
    tiles = antennas // 128
    x = volume.reshape(t * 2, 2, tiles, 128).transpose(0, 2, 1, 3)
    w = steering.transpose(0, 1, 3, 2).reshape(2, 2 * beams, antennas)
    chunk = (64 - tap_total + 1) // 16 * 16
    depth = -(-4 * t // 16) * 16
    out_dims = (2, beams // per, 2, per, samples) if per % 8 == 0 else (2, beams, samples)
    return pl.pallas_call(
        functools.partial(k1_kernel, chunk),
        out_shape=jax.ShapeDtypeStruct(out_dims, jnp.float32),
        in_specs=[pl.BlockSpec(memory_space=pltpu.HBM)] * 3,
        out_specs=pl.BlockSpec(memory_space=pltpu.VMEM),
        scratch_shapes=[
            pltpu.VMEM((tiles, depth // 2, 2, 128), jnp.bfloat16),
            pltpu.VMEM((2, 2 * beams, antennas), jnp.bfloat16),
            pltpu.VMEM((2, 2, samples, antennas), jnp.bfloat16),
            pltpu.SMEM((2, tap_total), jnp.float32),
            pltpu.SemaphoreType.DMA((tiles,)),
            pltpu.SemaphoreType.DMA,
            pltpu.SemaphoreType.DMA,
        ],
        compiler_params=pltpu.CompilerParams(vmem_limit_bytes=67043328),
        name="channelize",
    )(taps.T, x, w)


UNROLL = 128
RAMPS = 4


def merge_table(offsets, boxes, half, block, per):
    levels, _, delays = offsets.shape
    row = jnp.arange(delays, dtype=jnp.int32)
    parts = []
    for level in range(levels):
        child = delays >> (levels - level)
        base = row & ~(2 * child - 1)
        low, high = offsets[level, 0], offsets[level, 1]
        part = jnp.stack([(base + low) * per, (base + child + high) * per, low])
        if level == levels - 1:
            near, far = part[:, : delays // 2], part[:, delays // 2 :]
            part = jnp.where(half == 0, jnp.concatenate([near, far], 1), jnp.concatenate([far, near], 1))
        parts.append(part)
    table = jnp.stack(parts).reshape(-1)
    tail = jnp.concatenate([boxes, jnp.full((1,), block, jnp.int32)])
    return jnp.concatenate([table, jnp.pad(tail, (0, 128 - tail.shape[0]))])


def repeat(count, body):
    if count == 1:
        body(0, 0)
    else:
        lax.fori_loop(0, count, body, 0)


def split_lanes(value):
    return [value[:, 128 * t : 128 * t + 128] for t in range(value.shape[-1] // 128)]


def shifted(pieces, amount, limit):
    lane = lax.broadcasted_iota(jnp.int32, pieces[0].shape, 1)
    zero = jnp.zeros_like(pieces[0])
    tiles = len(pieces)
    rest = amount
    if limit > 128:
        whole = amount >> 7
        rest = amount & 127
        moved = []
        for t in range(tiles):
            piece = zero
            for q in range(t + 1):
                piece = jnp.where(whole == q, pieces[t - q], piece)
            moved.append(piece)
        pieces = moved
    rolled = [pltpu.roll(piece, rest, 1) for piece in pieces]
    kept = lane >= rest
    return [jnp.where(kept, rolled[t], rolled[t - 1] if t else zero) for t in range(tiles)]


def k2_kernel(
    table_hbm, normed_ref, dedispersed_ref, scores_ref, peak_ref,
    plane_a, plane_b, own, other, *rest_refs,
):
    *ramps, tops, table_ref, table_sem, out_sem = rest_refs
    planes = (plane_a, plane_b)
    channels, per, samples = normed_ref.shape
    delays = plane_a.shape[1] // per
    tiles = samples // 128
    rate = delays // channels
    levels = (table_ref.shape[0] - 128) // (3 * delays)
    half_rows = delays // 2
    box_total = scores_ref.shape[0]
    tail = 3 * delays * levels
    table_copy = pltpu.make_async_copy(table_hbm, table_ref, table_sem)
    table_copy.start()
    for ramp in ramps:
        ramp[pl.ds(0, samples), :] = jnp.zeros((samples, 128), jnp.float32)
    total = normed_ref[0]
    for c in range(1, channels):
        total = total + normed_ref[c]
    common = total * (1.0 / channels)

    group = min(4, channels)

    def put(level, t, row, value):
        rows = pl.ds(row * per if isinstance(row, int) else pl.multiple_of(row * per, per), per)
        planes[level % 2][t, rows, :] = value

    def first(i, carry):
        terms = []
        for u in range(group):
            cleaned = split_lanes(normed_ref[group * i + u] - common)
            running = cleaned
            terms.append(running)
            for lag in range(1, rate):
                running = [a + b for a, b in zip(running, shifted(cleaned, lag, 1))]
                terms.append(running)
        for u in range(group * rate):
            for t in range(tiles):
                put(0, t, group * rate * i + u, terms[u][t])
        return carry

    lax.fori_loop(0, channels // group, first, 0)
    table_copy.wait()

    def merged(level, row):
        start = 3 * delays * level
        lower = table_ref[start + row]
        upper = table_ref[start + delays + row]
        low = table_ref[start + 2 * delays + row]
        source = planes[level % 2]
        lower_rows = pl.ds(pl.multiple_of(lower, per), per)
        upper_rows = pl.ds(pl.multiple_of(upper, per), per)
        moved = shifted([source[t, upper_rows, :] for t in range(tiles)], low, rate << level)
        return [source[t, lower_rows, :] + moved[t] for t in range(tiles)]

    for level in range(levels - 1):
        def one(i, carry, level=level):
            for u in range(UNROLL):
                row = merged(level, UNROLL * i + u)
                for t in range(tiles):
                    put(level + 1, t, UNROLL * i + u, row[t])
            return carry
        repeat(delays // UNROLL, one)

    scale = 1.0 / math.sqrt(channels)
    step = 8
    span = min(UNROLL, half_rows)
    for k in range(2):
        target = own if k == 0 else other
        def last(i, carry, k=k, target=target):
            for v in range(span // step):
                place = span * i + step * v
                rows = [jnp.concatenate(merged(levels - 1, k * half_rows + place + u), 1) * scale for u in range(step)]
                if per % 8 == 0:
                    target[:, pl.ds(place if isinstance(place, int) else pl.multiple_of(place, step), step), :] = jnp.transpose(jnp.stack(rows, 0), (1, 0, 2))
                else:
                    for u in range(step):
                        for b in range(per):
                            target[b, pl.ds(place + u, 1), :] = rows[u][b : b + 1]
            return carry
        repeat(half_rows // span, last)

    out_copy = pltpu.make_async_copy(own, dedispersed_ref, out_sem)
    out_copy.start()
    width = per * half_rows
    groups = width // 128
    head = samples // 2
    later = lax.broadcasted_iota(jnp.int32, (head, head), 0)
    earlier = lax.broadcasted_iota(jnp.int32, (head, head), 1)
    upto = jnp.where(earlier <= later, 1.0, 0.0).astype(jnp.bfloat16)
    upto = jnp.concatenate([upto] * 3, 1)
    spot = lax.broadcasted_iota(jnp.int32, (box_total, 128), 0)
    lengths = jnp.zeros((box_total, 128), jnp.int32)
    for w in range(box_total):
        lengths = jnp.where(spot == w, table_ref[tail + w], lengths)
    roots = jnp.sqrt(lengths.astype(jnp.float32))
    flat = [own.reshape(width, samples), other.reshape(width, samples)]
    block_rows = 64

    def sums(g, k):
        rows = flat[k][pl.ds(128 * g, 128), :]
        rest = jnp.concatenate([rows[:, :head], rows[:, head:]], 0)
        parts = []
        for piece in range(3):
            parts.append(rest.astype(jnp.bfloat16))
            if piece < 2:
                rest = rest - parts[-1].astype(jnp.float32)
        got = lax.dot_general(
            upto, jnp.concatenate(parts, 1), (((1,), (1,)), ((), ())), preferred_element_type=jnp.float32
        )
        ramp = ramps[(2 * g + k) % len(ramps)]
        ramp[pl.ds(samples, head), :] = got[:, :128]
        ramp[pl.ds(samples + head, head), :] = got[:, 128:] + got[head - 1 :, :128]

    def boxes(g, k):
        ramp = ramps[(2 * g + k) % len(ramps)]
        best = [None] * box_total
        for s0 in range(0, samples, block_rows):
            here = ramp[pl.ds(samples + s0, block_rows), :]
            for w in range(box_total):
                response = here - ramp[pl.ds(samples + s0 - table_ref[tail + w], block_rows), :]
                found = jnp.max(response.reshape(block_rows // 8, 8, 128), axis=0)
                best[w] = found if best[w] is None else jnp.maximum(best[w], found)
        scores = jnp.concatenate([jnp.max(b, axis=0, keepdims=True) for b in best], 0) / roots
        if k == 0:
            scores_ref[:, pl.ds(128 * g, 128)] = scores
        tops[pl.ds(k * groups + g, 1), :] = jnp.max(scores, axis=0, keepdims=True)

    order = [(g, k) for k in range(2) for g in range(groups)]
    sums(*order[0])
    for n, spot_now in enumerate(order):
        if n + 1 < len(order):
            sums(*order[n + 1])
        boxes(*spot_now)
    block = table_ref[tail + box_total]
    values = tops[...]
    lane = lax.broadcasted_iota(jnp.int32, values.shape, 1)
    place = lax.broadcasted_iota(jnp.int32, values.shape, 0)
    place = 128 * jnp.where(place >= groups, place - groups, place)
    peaks = jnp.full(values.shape, -jnp.inf, jnp.float32)
    span = min(half_rows, 128)
    for q in range(128 // span):
        inside = (lane >= span * q) & (lane < span * (q + 1))
        top = jnp.max(jnp.where(inside, values, -jnp.inf), axis=1, keepdims=True)
        beam = block * per + (place + span * q) // half_rows
        peaks = jnp.where(lane == beam, jnp.maximum(top, peaks), peaks)
    peak_ref[...] = jnp.max(peaks, axis=0, keepdims=True)[:, : peak_ref.shape[1]]
    out_copy.wait()


def k2(table, normed, beams, delays, box_total):
    channels, per, samples = normed.shape
    half_rows = delays // 2
    groups = per * half_rows // 128
    vmem = pl.BlockSpec(memory_space=pltpu.VMEM)
    hbm = pl.BlockSpec(memory_space=pl.ANY)
    return pl.pallas_call(
        k2_kernel,
        out_shape=(
            jax.ShapeDtypeStruct((per, half_rows, samples), jnp.float32),
            jax.ShapeDtypeStruct((box_total, per * half_rows), jnp.float32),
            jax.ShapeDtypeStruct((1, beams), jnp.float32),
        ),
        in_specs=[hbm, vmem],
        out_specs=(hbm, vmem, vmem),
        scratch_shapes=[
            *[pltpu.VMEM((samples // 128, delays * per, 128), jnp.float32)] * 2,
            *[pltpu.VMEM((per, half_rows, samples), jnp.float32)] * 2,
            *[pltpu.VMEM((2 * samples, 128), jnp.float32)] * RAMPS,
            pltpu.VMEM((2 * groups, 128), jnp.float32),
            pltpu.SMEM(table.shape, jnp.int32),
            pltpu.SemaphoreType.DMA,
            pltpu.SemaphoreType.DMA,
        ],
        compiler_params=pltpu.CompilerParams(vmem_limit_bytes=48 << 20),
        name="dedisperse",
    )(table, normed)


def shards(voltages, pfb_taps, steering, fdmt_offsets, box_lengths):
    devices = lax.axis_size("freq")
    device_id = lax.axis_index("freq")
    beams = steering.shape[-1]
    blocks = devices // 2
    per = beams // blocks
    samples = voltages.shape[1] - pfb_taps.shape[0] + 1
    normed = k1(pfb_taps, voltages[0], steering, per)
    if normed.ndim == 3:
        normed = normed.reshape(2, blocks, per, samples).transpose(1, 0, 2, 3)
        normed = jnp.broadcast_to(normed[None], (2,) + normed.shape)
    outgoing = normed.reshape(devices, 2, per, samples)
    incoming = lax.all_to_all(outgoing, "freq", split_axis=0, concat_axis=0, tiled=True)
    table = merge_table(fdmt_offsets, box_lengths, device_id // blocks, device_id % blocks, per)
    delays, box_total = fdmt_offsets.shape[-1], box_lengths.shape[0]
    dedispersed, box_scores, peaks = k2(
        table, incoming.reshape(2 * devices, per, samples), beams, delays, box_total
    )
    box_scores = box_scores.reshape(box_total, per, delays // 2).transpose(1, 0, 2)
    step = 1
    while step < blocks:
        pairs = [(spot, spot ^ step) for spot in range(devices)]
        peaks = jnp.maximum(peaks, lax.ppermute(peaks, "freq", pairs))
        step *= 2
    return (dedispersed, box_scores, peaks.reshape(beams))


def solution(mesh):
    placed = (
        P(("groups", "freq"), None, None, None, None),
        P(),
        P(("groups", "freq"), None, None, None),
        P(),
        P(),
    )
    return jax.shard_map(
        shards,
        mesh=mesh,
        in_specs=placed,
        out_specs=(
            P(("groups", "freq"), None, None),
            P(("groups", "freq"), None, None),
            P("groups"),
        ),
        check_vma=False,
    )
```

```python
import functools
import math

import jax
import jax.numpy as jnp
from jax import lax
from jax.experimental import pallas as pl
from jax.experimental.pallas import tpu as pltpu
from jax.sharding import PartitionSpec as P


PAIRS = 4

def k1_kernel(chunk, taps_hbm, x_hbm, w_hbm, out_ref, slab, wbuf, fine, taps_ref, x_sem, w_sem, taps_sem):
    branches, tap_total = taps_ref.shape
    rows_in, tiles = x_hbm.shape[0], x_hbm.shape[1]
    samples = fine.shape[2]
    beams2 = wbuf.shape[1]
    beams = beams2 // 2
    flat = slab.reshape(tiles, 2 * slab.shape[1], 128)
    window = -(-4 * (chunk + tap_total - 1) // 16) * 16

    def x_copy(j):
        return pltpu.make_async_copy(x_hbm.at[:, j], slab.at[j, pl.ds(0, rows_in)], x_sem.at[j])

    taps_copy = pltpu.make_async_copy(taps_hbm, taps_ref, taps_sem)
    taps_copy.start()
    for j in range(tiles):
        x_copy(j).start()
    w_copy = pltpu.make_async_copy(w_hbm, wbuf, w_sem)
    w_copy.start()
    taps_copy.wait()
    shape = (2, 2, chunk, window)
    col = lax.broadcasted_iota(jnp.int32, shape, 3)
    part = lax.broadcasted_iota(jnp.int32, shape, 0)
    fsel = lax.broadcasted_iota(jnp.int32, shape, 1)
    tap = (col >> 2) - lax.broadcasted_iota(jnp.int32, shape, 2)
    branch = (col >> 1) & 1
    code = jnp.where((col & 1) == part, tap * 2 + branch, -1)
    weights = jnp.zeros(shape, jnp.float32)
    for k in range(tap_total):
        for p in range(branches):
            weights = jnp.where(code == 2 * k + p, taps_ref[p, k], weights)
    weights = jnp.where((fsel & branch) == 1, -weights, weights).reshape(4 * chunk, window)
    high = weights.astype(jnp.bfloat16)
    low = (weights - high.astype(jnp.float32)).astype(jnp.bfloat16)
    spans = [(s0, min(chunk, samples - s0)) for s0 in range(0, samples, chunk)]
    spans = [(s0, size, -(-4 * (size + tap_total - 1) // 16) * 16) for s0, size in spans]
    filters = {}
    for _, size, reach in spans:
        if size not in filters:
            filters[size] = jnp.concatenate(
                [part[q * chunk : q * chunk + size, :reach] for part in (high, low) for q in range(4)], 0
            )

    def load(g, s0, size, reach):
        pieces = [flat[2 * g + i, pl.ds(4 * s0, reach), :] for i in range(2)]
        return jnp.concatenate(pieces, 1)

    def pairs(h, carry):
        work = []
        for u in range(PAIRS):
            g = PAIRS * h + u
            work += [(g, *span) for span in spans]
        for u in range(PAIRS):
            x_copy(2 * (PAIRS * h + u)).wait()
            x_copy(2 * (PAIRS * h + u) + 1).wait()
        ahead = load(*work[0])
        for n, (g, s0, size, _) in enumerate(work):
            here = ahead
            if n + 1 < len(work):
                ahead = load(*work[n + 1])
            got = jnp.dot(filters[size], here, preferred_element_type=jnp.float32)
            rounded = (got[: 4 * size] + got[4 * size :]).astype(jnp.bfloat16)
            for q in range(4):
                fine[q // 2, q % 2, pl.ds(s0, size), pl.ds(pl.multiple_of(256 * g, 256), 256)] = rounded[
                    q * size : (q + 1) * size
                ]
        return carry

    for j in range(tiles):
        spare = slab.shape[1] - rows_in
        if spare:
            slab[j, pl.ds(rows_in, spare)] = jnp.zeros((spare, 2, 128), jnp.bfloat16)
    lax.fori_loop(0, tiles // 2 // PAIRS, pairs, 0)
    w_copy.wait()
    for f in range(2):
        dims = (((1,), (1,)), ((), ()))
        got_re = lax.dot_general(fine[0, f], wbuf[f], dims, preferred_element_type=jnp.float32).T
        got_im = lax.dot_general(fine[1, f], wbuf[f], dims, preferred_element_type=jnp.float32).T
        beam_re = got_re[:beams] - got_im[beams:]
        beam_im = got_re[beams:] + got_im[:beams]
        power = beam_re * beam_re + beam_im * beam_im
        level = jnp.mean(power, axis=-1, keepdims=True)
        centered = power - level
        spread = jnp.mean(centered * centered, axis=-1, keepdims=True)
        normed = centered / jnp.sqrt(spread + 1e-05)
        if out_ref.ndim == 5:
            normed = normed.reshape(out_ref.shape[1], out_ref.shape[3], samples)
            for h in range(2):
                out_ref[h, :, f] = normed
        else:
            out_ref[f] = normed

def k1(taps, volume, steering, per):
    t, branches, parts, antennas = volume.shape
    tap_total = taps.shape[0]
    samples = t - tap_total + 1
    beams = steering.shape[-1]
    tiles = antennas // 128
    x = volume.reshape(t * 2, 2, tiles, 128).transpose(0, 2, 1, 3)
    w = steering.transpose(0, 1, 3, 2).reshape(2, 2 * beams, antennas)
    chunk = (64 - tap_total + 1) // 16 * 16
    depth = -(-4 * t // 16) * 16
    out_dims = (2, beams // per, 2, per, samples) if per % 8 == 0 else (2, beams, samples)
    return pl.pallas_call(
        functools.partial(k1_kernel, chunk),
        out_shape=jax.ShapeDtypeStruct(out_dims, jnp.float32),
        in_specs=[pl.BlockSpec(memory_space=pltpu.HBM)] * 3,
        out_specs=pl.BlockSpec(memory_space=pltpu.VMEM),
        scratch_shapes=[
            pltpu.VMEM((tiles, depth // 2, 2, 128), jnp.bfloat16),
            pltpu.VMEM((2, 2 * beams, antennas), jnp.bfloat16),
            pltpu.VMEM((2, 2, samples, antennas), jnp.bfloat16),
            pltpu.SMEM((2, tap_total), jnp.float32),
            pltpu.SemaphoreType.DMA((tiles,)),
            pltpu.SemaphoreType.DMA,
            pltpu.SemaphoreType.DMA,
        ],
        compiler_params=pltpu.CompilerParams(vmem_limit_bytes=67043328),
        name="channelize",
    )(taps.T, x, w)


UNROLL = 128
RAMPS = 4


def merge_table(offsets, boxes, half, block, per):
    levels, _, delays = offsets.shape
    row = jnp.arange(delays, dtype=jnp.int32)
    parts = []
    for level in range(levels):
        child = delays >> (levels - level)
        base = row & ~(2 * child - 1)
        low, high = offsets[level, 0], offsets[level, 1]
        part = jnp.stack([(base + low) * per, (base + child + high) * per, low])
        if level == levels - 1:
            near, far = part[:, : delays // 2], part[:, delays // 2 :]
            part = jnp.where(half == 0, jnp.concatenate([near, far], 1), jnp.concatenate([far, near], 1))
        parts.append(part)
    table = jnp.stack(parts).reshape(-1)
    tail = jnp.concatenate([boxes, jnp.full((1,), block, jnp.int32)])
    return jnp.concatenate([table, jnp.pad(tail, (0, 128 - tail.shape[0]))])


def repeat(count, body):
    if count == 1:
        body(0, 0)
    else:
        lax.fori_loop(0, count, body, 0)


def split_lanes(value):
    return [value[:, 128 * t : 128 * t + 128] for t in range(value.shape[-1] // 128)]


def shifted(pieces, amount, limit):
    lane = lax.broadcasted_iota(jnp.int32, pieces[0].shape, 1)
    zero = jnp.zeros_like(pieces[0])
    tiles = len(pieces)
    rest = amount
    if limit > 128:
        whole = amount >> 7
        rest = amount & 127
        moved = []
        for t in range(tiles):
            piece = zero
            for q in range(t + 1):
                piece = jnp.where(whole == q, pieces[t - q], piece)
            moved.append(piece)
        pieces = moved
    rolled = [pltpu.roll(piece, rest, 1) for piece in pieces]
    kept = lane >= rest
    return [jnp.where(kept, rolled[t], rolled[t - 1] if t else zero) for t in range(tiles)]


def k2_kernel(
    table_hbm, normed_ref, dedispersed_ref, scores_ref, peak_ref,
    plane_a, plane_b, own, other, *rest_refs,
):
    *ramps, tops, table_ref, table_sem, out_sem = rest_refs
    planes = (plane_a, plane_b)
    channels, per, samples = normed_ref.shape
    delays = plane_a.shape[1] // per
    tiles = samples // 128
    rate = delays // channels
    levels = (table_ref.shape[0] - 128) // (3 * delays)
    half_rows = delays // 2
    box_total = scores_ref.shape[0]
    tail = 3 * delays * levels
    table_copy = pltpu.make_async_copy(table_hbm, table_ref, table_sem)
    table_copy.start()
    for ramp in ramps:
        ramp[pl.ds(0, samples), :] = jnp.zeros((samples, 128), jnp.float32)
    total = normed_ref[0]
    for c in range(1, channels):
        total = total + normed_ref[c]
    common = total * (1.0 / channels)

    group = min(4, channels)

    def put(level, t, row, value):
        rows = pl.ds(row * per if isinstance(row, int) else pl.multiple_of(row * per, per), per)
        planes[level % 2][t, rows, :] = value

    def first(i, carry):
        terms = []
        for u in range(group):
            cleaned = split_lanes(normed_ref[group * i + u] - common)
            running = cleaned
            terms.append(running)
            for lag in range(1, rate):
                running = [a + b for a, b in zip(running, shifted(cleaned, lag, 1))]
                terms.append(running)
        for u in range(group * rate):
            for t in range(tiles):
                put(0, t, group * rate * i + u, terms[u][t])
        return carry

    lax.fori_loop(0, channels // group, first, 0)
    table_copy.wait()

    def merged(level, row):
        start = 3 * delays * level
        lower = table_ref[start + row]
        upper = table_ref[start + delays + row]
        low = table_ref[start + 2 * delays + row]
        source = planes[level % 2]
        lower_rows = pl.ds(pl.multiple_of(lower, per), per)
        upper_rows = pl.ds(pl.multiple_of(upper, per), per)
        moved = shifted([source[t, upper_rows, :] for t in range(tiles)], low, rate << level)
        return [source[t, lower_rows, :] + moved[t] for t in range(tiles)]

    for level in range(levels - 1):
        def one(i, carry, level=level):
            for u in range(UNROLL):
                row = merged(level, UNROLL * i + u)
                for t in range(tiles):
                    put(level + 1, t, UNROLL * i + u, row[t])
            return carry
        repeat(delays // UNROLL, one)

    scale = 1.0 / math.sqrt(channels)
    step = 8
    span = min(UNROLL, half_rows)
    for k in range(2):
        target = own if k == 0 else other
        def last(i, carry, k=k, target=target):
            for v in range(span // step):
                place = span * i + step * v
                rows = [jnp.concatenate(merged(levels - 1, k * half_rows + place + u), 1) * scale for u in range(step)]
                if per % 8 == 0:
                    target[:, pl.ds(place if isinstance(place, int) else pl.multiple_of(place, step), step), :] = jnp.transpose(jnp.stack(rows, 0), (1, 0, 2))
                else:
                    for u in range(step):
                        for b in range(per):
                            target[b, pl.ds(place + u, 1), :] = rows[u][b : b + 1]
            return carry
        repeat(half_rows // span, last)

    out_copy = pltpu.make_async_copy(own, dedispersed_ref, out_sem)
    out_copy.start()
    width = per * half_rows
    groups = width // 128
    head = samples // 2
    later = lax.broadcasted_iota(jnp.int32, (head, head), 0)
    earlier = lax.broadcasted_iota(jnp.int32, (head, head), 1)
    upto = jnp.where(earlier <= later, 1.0, 0.0).astype(jnp.bfloat16)
    upto = jnp.concatenate([upto] * 3, 1)
    spot = lax.broadcasted_iota(jnp.int32, (box_total, 128), 0)
    lengths = jnp.zeros((box_total, 128), jnp.int32)
    for w in range(box_total):
        lengths = jnp.where(spot == w, table_ref[tail + w], lengths)
    roots = jnp.sqrt(lengths.astype(jnp.float32))
    flat = [own.reshape(width, samples), other.reshape(width, samples)]
    block_rows = 64

    def sums(g, k):
        rows = flat[k][pl.ds(128 * g, 128), :]
        rest = jnp.concatenate([rows[:, :head], rows[:, head:]], 0)
        parts = []
        for piece in range(3):
            parts.append(rest.astype(jnp.bfloat16))
            if piece < 2:
                rest = rest - parts[-1].astype(jnp.float32)
        got = lax.dot_general(
            upto, jnp.concatenate(parts, 1), (((1,), (1,)), ((), ())), preferred_element_type=jnp.float32
        )
        ramp = ramps[(2 * g + k) % len(ramps)]
        ramp[pl.ds(samples, head), :] = got[:, :128]
        ramp[pl.ds(samples + head, head), :] = got[:, 128:] + got[head - 1 :, :128]

    def boxes(g, k):
        ramp = ramps[(2 * g + k) % len(ramps)]
        best = [None] * box_total
        for s0 in range(0, samples, block_rows):
            here = ramp[pl.ds(samples + s0, block_rows), :]
            for w in range(box_total):
                response = here - ramp[pl.ds(samples + s0 - table_ref[tail + w], block_rows), :]
                found = jnp.max(response.reshape(block_rows // 8, 8, 128), axis=0)
                best[w] = found if best[w] is None else jnp.maximum(best[w], found)
        scores = jnp.concatenate([jnp.max(b, axis=0, keepdims=True) for b in best], 0) / roots
        if k == 0:
            scores_ref[:, pl.ds(128 * g, 128)] = scores
        tops[pl.ds(k * groups + g, 1), :] = jnp.max(scores, axis=0, keepdims=True)

    order = [(g, k) for k in range(2) for g in range(groups)]
    sums(*order[0])
    for n, spot_now in enumerate(order):
        if n + 1 < len(order):
            sums(*order[n + 1])
        boxes(*spot_now)
    block = table_ref[tail + box_total]
    values = tops[...]
    lane = lax.broadcasted_iota(jnp.int32, values.shape, 1)
    place = lax.broadcasted_iota(jnp.int32, values.shape, 0)
    place = 128 * jnp.where(place >= groups, place - groups, place)
    peaks = jnp.full(values.shape, -jnp.inf, jnp.float32)
    span = min(half_rows, 128)
    for q in range(128 // span):
        inside = (lane >= span * q) & (lane < span * (q + 1))
        top = jnp.max(jnp.where(inside, values, -jnp.inf), axis=1, keepdims=True)
        beam = block * per + (place + span * q) // half_rows
        peaks = jnp.where(lane == beam, jnp.maximum(top, peaks), peaks)
    peak_ref[...] = jnp.max(peaks, axis=0, keepdims=True)[:, : peak_ref.shape[1]]
    out_copy.wait()


def k2(table, normed, beams, delays, box_total):
    channels, per, samples = normed.shape
    half_rows = delays // 2
    groups = per * half_rows // 128
    vmem = pl.BlockSpec(memory_space=pltpu.VMEM)
    hbm = pl.BlockSpec(memory_space=pl.ANY)
    return pl.pallas_call(
        k2_kernel,
        out_shape=(
            jax.ShapeDtypeStruct((per, half_rows, samples), jnp.float32),
            jax.ShapeDtypeStruct((box_total, per * half_rows), jnp.float32),
            jax.ShapeDtypeStruct((1, beams), jnp.float32),
        ),
        in_specs=[hbm, vmem],
        out_specs=(hbm, vmem, vmem),
        scratch_shapes=[
            *[pltpu.VMEM((samples // 128, delays * per, 128), jnp.float32)] * 2,
            *[pltpu.VMEM((per, half_rows, samples), jnp.float32)] * 2,
            *[pltpu.VMEM((2 * samples, 128), jnp.float32)] * RAMPS,
            pltpu.VMEM((2 * groups, 128), jnp.float32),
            pltpu.SMEM(table.shape, jnp.int32),
            pltpu.SemaphoreType.DMA,
            pltpu.SemaphoreType.DMA,
        ],
        compiler_params=pltpu.CompilerParams(vmem_limit_bytes=48 << 20),
        name="dedisperse",
    )(table, normed)


def shards(voltages, pfb_taps, steering, fdmt_offsets, box_lengths):
    devices = lax.axis_size("freq")
    device_id = lax.axis_index("freq")
    beams = steering.shape[-1]
    blocks = devices // 2
    per = beams // blocks
    samples = voltages.shape[1] - pfb_taps.shape[0] + 1
    normed = k1(pfb_taps, voltages[0], steering, per)
    if normed.ndim == 3:
        normed = normed.reshape(2, blocks, per, samples).transpose(1, 0, 2, 3)
        normed = jnp.broadcast_to(normed[None], (2,) + normed.shape)
    outgoing = normed.reshape(devices, 2, per, samples)
    incoming = lax.all_to_all(outgoing, "freq", split_axis=0, concat_axis=0, tiled=True)
    table = merge_table(fdmt_offsets, box_lengths, device_id // blocks, device_id % blocks, per)
    delays, box_total = fdmt_offsets.shape[-1], box_lengths.shape[0]
    dedispersed, box_scores, peaks = k2(
        table, incoming.reshape(2 * devices, per, samples), beams, delays, box_total
    )
    box_scores = box_scores.reshape(box_total, per, delays // 2).transpose(1, 0, 2)
    steps = [1 << bit for bit in range(1, blocks.bit_length() - 1)]
    phases = [(a, b, a + b) for a, b in zip(steps[::2], steps[1::2])]
    phases += [(step,) for step in steps[len(phases) * 2 :]] + [(1,)]
    for phase in phases if blocks > 1 else []:
        arrived = [
            lax.ppermute(peaks, "freq", [(spot, spot ^ step) for spot in range(devices)]) for step in phase
        ]
        for piece in arrived:
            peaks = jnp.maximum(peaks, piece)
    return (dedispersed, box_scores, peaks.reshape(beams))


def solution(mesh):
    placed = (
        P(("groups", "freq"), None, None, None, None),
        P(),
        P(("groups", "freq"), None, None, None),
        P(),
        P(),
    )
    return jax.shard_map(
        shards,
        mesh=mesh,
        in_specs=placed,
        out_specs=(
            P(("groups", "freq"), None, None),
            P(("groups", "freq"), None, None),
            P("groups"),
        ),
        check_vma=False,
    )
```

```python
import functools
import math

import jax
import jax.numpy as jnp
from jax import lax
from jax.experimental import pallas as pl
from jax.experimental.pallas import tpu as pltpu
from jax.sharding import PartitionSpec as P


def k1_kernel(chunk, taps_hbm, x_hbm, w_hbm, out_ref, slab, wbuf, fine, taps_ref, x_sem, w_sem, taps_sem):
    branches, tap_total = taps_ref.shape
    rows_in, tiles = x_hbm.shape[0], x_hbm.shape[1]
    samples = fine.shape[2]
    beams2 = wbuf.shape[1]
    beams = beams2 // 2
    flat = slab.reshape(tiles, 2 * slab.shape[1], 128)
    window = -(-4 * (chunk + tap_total - 1) // 16) * 16

    def x_copy(j):
        return pltpu.make_async_copy(x_hbm.at[:, j], slab.at[j, pl.ds(0, rows_in)], x_sem.at[j])

    taps_copy = pltpu.make_async_copy(taps_hbm, taps_ref, taps_sem)
    taps_copy.start()
    for j in range(tiles):
        x_copy(j).start()
    w_copy = pltpu.make_async_copy(w_hbm, wbuf, w_sem)
    w_copy.start()
    taps_copy.wait()
    shape = (2, 2, chunk, window)
    col = lax.broadcasted_iota(jnp.int32, shape, 3)
    part = lax.broadcasted_iota(jnp.int32, shape, 0)
    fsel = lax.broadcasted_iota(jnp.int32, shape, 1)
    tap = (col >> 2) - lax.broadcasted_iota(jnp.int32, shape, 2)
    branch = (col >> 1) & 1
    code = jnp.where((col & 1) == part, tap * 2 + branch, -1)
    weights = jnp.zeros(shape, jnp.float32)
    for k in range(tap_total):
        for p in range(branches):
            weights = jnp.where(code == 2 * k + p, taps_ref[p, k], weights)
    weights = jnp.where((fsel & branch) == 1, -weights, weights).reshape(4 * chunk, window)
    high = weights.astype(jnp.bfloat16)
    low = (weights - high.astype(jnp.float32)).astype(jnp.bfloat16)
    spans = [(s0, min(chunk, samples - s0)) for s0 in range(0, samples, chunk)]
    spans = [(s0, size, -(-4 * (size + tap_total - 1) // 16) * 16) for s0, size in spans]
    filters = {}
    for _, size, reach in spans:
        if size not in filters:
            filters[size] = jnp.concatenate(
                [part[q * chunk : q * chunk + size, :reach] for part in (high, low) for q in range(4)], 0
            )

    def load(g, s0, size, reach):
        pieces = [flat[2 * g + i, pl.ds(4 * s0, reach), :] for i in range(2)]
        return jnp.concatenate(pieces, 1)

    def pairs(first, many):
        work = []
        for u in range(many):
            g = first + u
            work += [(g, *span) for span in spans]
        for u in range(2 * many):
            x_copy(2 * first + u).wait()
        ahead = load(*work[0])
        for n, (g, s0, size, _) in enumerate(work):
            here = ahead
            if n + 1 < len(work):
                ahead = load(*work[n + 1])
            got = jnp.dot(filters[size], here, preferred_element_type=jnp.float32)
            rounded = (got[: 4 * size] + got[4 * size :]).astype(jnp.bfloat16)
            for q in range(4):
                fine[q // 2, q % 2, pl.ds(s0, size), pl.ds(256 * g, 256)] = rounded[
                    q * size : (q + 1) * size
                ]

    for j in range(tiles):
        spare = slab.shape[1] - rows_in
        if spare:
            slab[j, pl.ds(rows_in, spare)] = jnp.zeros((spare, 2, 128), jnp.bfloat16)
    place = 0
    pair_total = tiles // 2
    for many in (1, pair_total // 2 - 1, pair_total - pair_total // 2):
        pairs(place, many)
        place += many
    w_copy.wait()
    for f in range(2):
        dims = (((1,), (1,)), ((), ()))
        got_re = lax.dot_general(fine[0, f], wbuf[f], dims, preferred_element_type=jnp.float32).T
        got_im = lax.dot_general(fine[1, f], wbuf[f], dims, preferred_element_type=jnp.float32).T
        beam_re = got_re[:beams] - got_im[beams:]
        beam_im = got_re[beams:] + got_im[:beams]
        power = beam_re * beam_re + beam_im * beam_im
        level = jnp.mean(power, axis=-1, keepdims=True)
        centered = power - level
        spread = jnp.mean(centered * centered, axis=-1, keepdims=True)
        normed = centered / jnp.sqrt(spread + 1e-05)
        if out_ref.ndim == 5:
            normed = normed.reshape(out_ref.shape[1], out_ref.shape[3], samples)
            for h in range(2):
                out_ref[h, :, f] = normed
        else:
            out_ref[f] = normed

def k1(taps, volume, steering, per):
    t, branches, parts, antennas = volume.shape
    tap_total = taps.shape[0]
    samples = t - tap_total + 1
    beams = steering.shape[-1]
    tiles = antennas // 128
    x = volume.reshape(t * 2, 2, tiles, 128).transpose(0, 2, 1, 3)
    w = steering.transpose(0, 1, 3, 2).reshape(2, 2 * beams, antennas)
    chunk = (64 - tap_total + 1) // 16 * 16
    depth = -(-4 * t // 16) * 16
    out_dims = (2, beams // per, 2, per, samples) if per % 8 == 0 else (2, beams, samples)
    return pl.pallas_call(
        functools.partial(k1_kernel, chunk),
        out_shape=jax.ShapeDtypeStruct(out_dims, jnp.float32),
        in_specs=[pl.BlockSpec(memory_space=pltpu.HBM)] * 3,
        out_specs=pl.BlockSpec(memory_space=pltpu.VMEM),
        scratch_shapes=[
            pltpu.VMEM((tiles, depth // 2, 2, 128), jnp.bfloat16),
            pltpu.VMEM((2, 2 * beams, antennas), jnp.bfloat16),
            pltpu.VMEM((2, 2, samples, antennas), jnp.bfloat16),
            pltpu.SMEM((2, tap_total), jnp.float32),
            pltpu.SemaphoreType.DMA((tiles,)),
            pltpu.SemaphoreType.DMA,
            pltpu.SemaphoreType.DMA,
        ],
        compiler_params=pltpu.CompilerParams(vmem_limit_bytes=67043328),
        name="channelize",
    )(taps.T, x, w)


UNROLL = 128
RAMPS = 8


def merge_table(offsets, boxes, half, block, per):
    levels, _, delays = offsets.shape
    row = jnp.arange(delays, dtype=jnp.int32)
    parts = []
    for level in range(levels):
        child = delays >> (levels - level)
        base = row & ~(2 * child - 1)
        low, high = offsets[level, 0], offsets[level, 1]
        part = jnp.stack([(base + low) * per, (base + child + high) * per, low])
        if level == levels - 1:
            near, far = part[:, : delays // 2], part[:, delays // 2 :]
            part = jnp.where(half == 0, jnp.concatenate([near, far], 1), jnp.concatenate([far, near], 1))
        parts.append(part)
    table = jnp.stack(parts).reshape(-1)
    tail = jnp.concatenate([boxes, jnp.full((1,), block, jnp.int32)])
    return jnp.concatenate([table, jnp.pad(tail, (0, 128 - tail.shape[0]))])


def repeat(count, body):
    if count == 1:
        body(0, 0)
    else:
        lax.fori_loop(0, count, body, 0)


def split_lanes(value):
    return [value[:, 128 * t : 128 * t + 128] for t in range(value.shape[-1] // 128)]


def shifted(pieces, amount, limit):
    lane = lax.broadcasted_iota(jnp.int32, pieces[0].shape, 1)
    zero = jnp.zeros_like(pieces[0])
    tiles = len(pieces)
    rest = amount
    if limit > 128:
        whole = amount >> 7
        rest = amount & 127
        moved = []
        for t in range(tiles):
            piece = zero
            for q in range(t + 1):
                piece = jnp.where(whole == q, pieces[t - q], piece)
            moved.append(piece)
        pieces = moved
    rolled = [pltpu.roll(piece, rest, 1) for piece in pieces]
    kept = lane >= rest
    return [jnp.where(kept, rolled[t], rolled[t - 1] if t else zero) for t in range(tiles)]


def k2_kernel(
    table_hbm, normed_ref, dedispersed_ref, scores_ref, peak_ref,
    plane_a, plane_b, own, other, *rest_refs,
):
    *ramps, tops, table_ref, table_sem, out_sem = rest_refs
    planes = (plane_a, plane_b)
    channels, per, samples = normed_ref.shape
    delays = plane_a.shape[1] // per
    tiles = samples // 128
    rate = delays // channels
    levels = (table_ref.shape[0] - 128) // (3 * delays)
    half_rows = delays // 2
    box_total = scores_ref.shape[0]
    tail = 3 * delays * levels
    table_copy = pltpu.make_async_copy(table_hbm, table_ref, table_sem)
    table_copy.start()
    for ramp in ramps:
        ramp[pl.ds(0, samples), :] = jnp.zeros((samples, 128), jnp.float32)
    total = normed_ref[0]
    for c in range(1, channels):
        total = total + normed_ref[c]
    common = total * (1.0 / channels)

    group = min(4, channels)

    def put(level, t, row, value):
        rows = pl.ds(row * per if isinstance(row, int) else pl.multiple_of(row * per, per), per)
        planes[level % 2][t, rows, :] = value

    def first(i, carry):
        terms = []
        for u in range(group):
            cleaned = split_lanes(normed_ref[group * i + u] - common)
            running = cleaned
            terms.append(running)
            for lag in range(1, rate):
                running = [a + b for a, b in zip(running, shifted(cleaned, lag, 1))]
                terms.append(running)
        for u in range(group * rate):
            for t in range(tiles):
                put(0, t, group * rate * i + u, terms[u][t])
        return carry

    lax.fori_loop(0, channels // group, first, 0)
    table_copy.wait()

    def merged(level, row):
        start = 3 * delays * level
        lower = table_ref[start + row]
        upper = table_ref[start + delays + row]
        low = table_ref[start + 2 * delays + row]
        source = planes[level % 2]
        lower_rows = pl.ds(pl.multiple_of(lower, per), per)
        upper_rows = pl.ds(pl.multiple_of(upper, per), per)
        moved = shifted([source[t, upper_rows, :] for t in range(tiles)], low, rate << level)
        return [source[t, lower_rows, :] + moved[t] for t in range(tiles)]

    for level in range(levels - 1):
        def one(i, carry, level=level):
            for u in range(UNROLL):
                row = merged(level, UNROLL * i + u)
                for t in range(tiles):
                    put(level + 1, t, UNROLL * i + u, row[t])
            return carry
        repeat(delays // UNROLL, one)

    scale = 1.0 / math.sqrt(channels)
    step = 8
    span = min(UNROLL, half_rows)
    for k in range(2):
        target = own if k == 0 else other
        def last(i, carry, k=k, target=target):
            for v in range(span // step):
                place = span * i + step * v
                rows = [jnp.concatenate(merged(levels - 1, k * half_rows + place + u), 1) * scale for u in range(step)]
                if per % 8 == 0:
                    target[:, pl.ds(place if isinstance(place, int) else pl.multiple_of(place, step), step), :] = jnp.transpose(jnp.stack(rows, 0), (1, 0, 2))
                else:
                    for u in range(step):
                        for b in range(per):
                            target[b, pl.ds(place + u, 1), :] = rows[u][b : b + 1]
            return carry
        repeat(half_rows // span, last)

    out_copy = pltpu.make_async_copy(own, dedispersed_ref, out_sem)
    out_copy.start()
    width = per * half_rows
    groups = width // 128
    head = samples // 2
    later = lax.broadcasted_iota(jnp.int32, (head, head), 0)
    earlier = lax.broadcasted_iota(jnp.int32, (head, head), 1)
    upto = jnp.where(earlier <= later, 1.0, 0.0).astype(jnp.bfloat16)
    upto = jnp.concatenate([upto] * 3, 1)
    spot = lax.broadcasted_iota(jnp.int32, (box_total, 128), 0)
    lengths = jnp.zeros((box_total, 128), jnp.int32)
    for w in range(box_total):
        lengths = jnp.where(spot == w, table_ref[tail + w], lengths)
    roots = jnp.sqrt(lengths.astype(jnp.float32))
    flat = [own.reshape(width, samples), other.reshape(width, samples)]
    block_rows = 64

    def sums(g, k):
        rows = flat[k][pl.ds(128 * g, 128), :]
        rest = jnp.concatenate([rows[:, :head], rows[:, head:]], 0)
        parts = []
        for piece in range(3):
            parts.append(rest.astype(jnp.bfloat16))
            if piece < 2:
                rest = rest - parts[-1].astype(jnp.float32)
        got = lax.dot_general(
            upto, jnp.concatenate(parts, 1), (((1,), (1,)), ((), ())), preferred_element_type=jnp.float32
        )
        ramp = ramps[(2 * g + k) % len(ramps)]
        ramp[pl.ds(samples, head), :] = got[:, :128]
        ramp[pl.ds(samples + head, head), :] = got[:, 128:] + got[head - 1 :, :128]

    def boxes(g, k):
        ramp = ramps[(2 * g + k) % len(ramps)]
        best = [None] * box_total
        for s0 in range(0, samples, block_rows):
            here = ramp[pl.ds(samples + s0, block_rows), :]
            for w in range(box_total):
                response = here - ramp[pl.ds(samples + s0 - table_ref[tail + w], block_rows), :]
                found = jnp.max(response.reshape(block_rows // 8, 8, 128), axis=0)
                best[w] = found if best[w] is None else jnp.maximum(best[w], found)
        scores = jnp.concatenate([jnp.max(b, axis=0, keepdims=True) for b in best], 0) / roots
        if k == 0:
            scores_ref[:, pl.ds(128 * g, 128)] = scores
        tops[pl.ds(k * groups + g, 1), :] = jnp.max(scores, axis=0, keepdims=True)

    order = [(g, k) for k in range(2) for g in range(groups)]
    sums(*order[0])
    for n, spot_now in enumerate(order):
        if n + 1 < len(order):
            sums(*order[n + 1])
        boxes(*spot_now)
    block = table_ref[tail + box_total]
    values = tops[...]
    lane = lax.broadcasted_iota(jnp.int32, values.shape, 1)
    place = lax.broadcasted_iota(jnp.int32, values.shape, 0)
    place = 128 * jnp.where(place >= groups, place - groups, place)
    peaks = jnp.full(values.shape, -jnp.inf, jnp.float32)
    span = min(half_rows, 128)
    for q in range(128 // span):
        inside = (lane >= span * q) & (lane < span * (q + 1))
        top = jnp.max(jnp.where(inside, values, -jnp.inf), axis=1, keepdims=True)
        beam = block * per + (place + span * q) // half_rows
        peaks = jnp.where(lane == beam, jnp.maximum(top, peaks), peaks)
    peak_ref[...] = jnp.max(peaks, axis=0, keepdims=True)[:, : peak_ref.shape[1]]
    out_copy.wait()


def k2(table, normed, beams, delays, box_total):
    channels, per, samples = normed.shape
    half_rows = delays // 2
    groups = per * half_rows // 128
    vmem = pl.BlockSpec(memory_space=pltpu.VMEM)
    hbm = pl.BlockSpec(memory_space=pl.ANY)
    return pl.pallas_call(
        k2_kernel,
        out_shape=(
            jax.ShapeDtypeStruct((per, half_rows, samples), jnp.float32),
            jax.ShapeDtypeStruct((box_total, per * half_rows), jnp.float32),
            jax.ShapeDtypeStruct((1, beams), jnp.float32),
        ),
        in_specs=[hbm, vmem],
        out_specs=(hbm, vmem, vmem),
        scratch_shapes=[
            *[pltpu.VMEM((samples // 128, delays * per, 128), jnp.float32)] * 2,
            *[pltpu.VMEM((per, half_rows, samples), jnp.float32)] * 2,
            *[pltpu.VMEM((2 * samples, 128), jnp.float32)] * RAMPS,
            pltpu.VMEM((2 * groups, 128), jnp.float32),
            pltpu.SMEM(table.shape, jnp.int32),
            pltpu.SemaphoreType.DMA,
            pltpu.SemaphoreType.DMA,
        ],
        compiler_params=pltpu.CompilerParams(vmem_limit_bytes=48 << 20),
        name="dedisperse",
    )(table, normed)


def shards(voltages, pfb_taps, steering, fdmt_offsets, box_lengths):
    devices = lax.axis_size("freq")
    device_id = lax.axis_index("freq")
    beams = steering.shape[-1]
    blocks = devices // 2
    per = beams // blocks
    samples = voltages.shape[1] - pfb_taps.shape[0] + 1
    normed = k1(pfb_taps, voltages[0], steering, per)
    if normed.ndim == 3:
        normed = normed.reshape(2, blocks, per, samples).transpose(1, 0, 2, 3)
        normed = jnp.broadcast_to(normed[None], (2,) + normed.shape)
    outgoing = normed.reshape(devices, 2, per, samples)
    incoming = lax.all_to_all(outgoing, "freq", split_axis=0, concat_axis=0, tiled=True)
    table = merge_table(fdmt_offsets, box_lengths, device_id // blocks, device_id % blocks, per)
    delays, box_total = fdmt_offsets.shape[-1], box_lengths.shape[0]
    dedispersed, box_scores, peaks = k2(
        table, incoming.reshape(2 * devices, per, samples), beams, delays, box_total
    )
    box_scores = box_scores.reshape(box_total, per, delays // 2).transpose(1, 0, 2)
    steps = [1 << bit for bit in range(1, blocks.bit_length() - 1)]
    phases = [(a, b, a + b) for a, b in zip(steps[::2], steps[1::2])]
    phases += [(step,) for step in steps[len(phases) * 2 :]] + [(1,)]
    for phase in phases if blocks > 1 else []:
        arrived = [
            lax.ppermute(peaks, "freq", [(spot, spot ^ step) for spot in range(devices)]) for step in phase
        ]
        for piece in arrived:
            peaks = jnp.maximum(peaks, piece)
    return (dedispersed, box_scores, peaks.reshape(beams))


def solution(mesh):
    placed = (
        P(("groups", "freq"), None, None, None, None),
        P(),
        P(("groups", "freq"), None, None, None),
        P(),
        P(),
    )
    return jax.shard_map(
        shards,
        mesh=mesh,
        in_specs=placed,
        out_specs=(
            P(("groups", "freq"), None, None),
            P(("groups", "freq"), None, None),
            P("groups"),
        ),
        check_vma=False,
    )
```

```python
import functools
import math

import jax
import jax.numpy as jnp
from jax import lax
from jax.experimental import pallas as pl
from jax.experimental.pallas import tpu as pltpu
from jax.sharding import PartitionSpec as P


def k1_kernel(chunk, taps_hbm, x_hbm, w_hbm, out_ref, slab, wbuf, fine, ready, taps_ref, x_sem, w_sem, taps_sem, out_sem):
    branches, tap_total = taps_ref.shape
    rows_in, tiles = x_hbm.shape[0], x_hbm.shape[1]
    samples = fine.shape[2]
    beams2 = wbuf.shape[1]
    beams = beams2 // 2
    flat = slab.reshape(tiles, 2 * slab.shape[1], 128)
    window = -(-4 * (chunk + tap_total - 1) // 16) * 16

    def x_copy(j):
        return pltpu.make_async_copy(x_hbm.at[:, j], slab.at[j, pl.ds(0, rows_in)], x_sem.at[j])

    taps_copy = pltpu.make_async_copy(taps_hbm, taps_ref, taps_sem)
    taps_copy.start()
    for j in range(tiles):
        x_copy(j).start()
    w_copy = pltpu.make_async_copy(w_hbm, wbuf, w_sem)
    w_copy.start()
    taps_copy.wait()
    shape = (2, 2, chunk, window)
    col = lax.broadcasted_iota(jnp.int32, shape, 3)
    part = lax.broadcasted_iota(jnp.int32, shape, 0)
    fsel = lax.broadcasted_iota(jnp.int32, shape, 1)
    tap = (col >> 2) - lax.broadcasted_iota(jnp.int32, shape, 2)
    branch = (col >> 1) & 1
    code = jnp.where((col & 1) == part, tap * 2 + branch, -1)
    weights = jnp.zeros(shape, jnp.float32)
    for k in range(tap_total):
        for p in range(branches):
            weights = jnp.where(code == 2 * k + p, taps_ref[p, k], weights)
    weights = jnp.where((fsel & branch) == 1, -weights, weights).reshape(4 * chunk, window)
    high = weights.astype(jnp.bfloat16)
    low = (weights - high.astype(jnp.float32)).astype(jnp.bfloat16)
    spans = [(s0, min(chunk, samples - s0)) for s0 in range(0, samples, chunk)]
    spans = [(s0, size, -(-4 * (size + tap_total - 1) // 16) * 16) for s0, size in spans]
    filters = {}
    for _, size, reach in spans:
        if size not in filters:
            filters[size] = jnp.concatenate(
                [part[q * chunk : q * chunk + size, :reach] for part in (high, low) for q in range(4)], 0
            )

    def load(g, s0, size, reach):
        pieces = [flat[2 * g + i, pl.ds(4 * s0, reach), :] for i in range(2)]
        return jnp.concatenate(pieces, 1)

    def pairs(first, many):
        work = []
        for u in range(many):
            g = first + u
            work += [(g, *span) for span in spans]
        for u in range(2 * many):
            x_copy(2 * first + u).wait()
        ahead = load(*work[0])
        for n, (g, s0, size, _) in enumerate(work):
            here = ahead
            if n + 1 < len(work):
                ahead = load(*work[n + 1])
            got = jnp.dot(filters[size], here, preferred_element_type=jnp.float32)
            rounded = (got[: 4 * size] + got[4 * size :]).astype(jnp.bfloat16)
            for q in range(4):
                fine[q // 2, q % 2, pl.ds(s0, size), pl.ds(256 * g, 256)] = rounded[
                    q * size : (q + 1) * size
                ]

    for j in range(tiles):
        spare = slab.shape[1] - rows_in
        if spare:
            slab[j, pl.ds(rows_in, spare)] = jnp.zeros((spare, 2, 128), jnp.bfloat16)
    place = 0
    pair_total = tiles // 2
    for many in (1, pair_total // 2 - 1, pair_total - pair_total // 2):
        pairs(place, many)
        place += many
    w_copy.wait()
    sends = []

    def spots(f):
        return [out_ref.at[h, :, f] for h in range(2)] if len(out_ref.shape) == 5 else [out_ref.at[f]]

    for f in range(2):
        dims = (((1,), (1,)), ((), ()))
        got_re = lax.dot_general(fine[0, f], wbuf[f], dims, preferred_element_type=jnp.float32).T
        got_im = lax.dot_general(fine[1, f], wbuf[f], dims, preferred_element_type=jnp.float32).T
        beam_re = got_re[:beams] - got_im[beams:]
        beam_im = got_re[beams:] + got_im[:beams]
        power = beam_re * beam_re + beam_im * beam_im
        level = jnp.mean(power, axis=-1, keepdims=True)
        centered = power - level
        spread = jnp.mean(centered * centered, axis=-1, keepdims=True)
        normed = centered / jnp.sqrt(spread + 1e-05)
        ready[f] = normed.reshape(ready.shape[1:])
        sends += [pltpu.make_async_copy(ready.at[f], spot, out_sem.at[len(sends) + n]) for n, spot in enumerate(spots(f))]
        for send in sends[-len(spots(f)) :]:
            send.start()
    for send in sends:
        send.wait()


def k1(taps, volume, steering, per):
    t, branches, parts, antennas = volume.shape
    tap_total = taps.shape[0]
    samples = t - tap_total + 1
    beams = steering.shape[-1]
    tiles = antennas // 128
    x = volume.reshape(t * 2, 2, tiles, 128).transpose(0, 2, 1, 3)
    w = steering.transpose(0, 1, 3, 2).reshape(2, 2 * beams, antennas)
    chunk = (64 - tap_total + 1) // 16 * 16
    depth = -(-4 * t // 16) * 16
    out_dims = (2, beams // per, 2, per, samples) if per % 8 == 0 else (2, beams, samples)
    return pl.pallas_call(
        functools.partial(k1_kernel, chunk),
        out_shape=jax.ShapeDtypeStruct(out_dims, jnp.float32),
        in_specs=[pl.BlockSpec(memory_space=pltpu.HBM)] * 3,
        out_specs=pl.BlockSpec(memory_space=pl.ANY),
        scratch_shapes=[
            pltpu.VMEM((tiles, depth // 2, 2, 128), jnp.bfloat16),
            pltpu.VMEM((2, 2 * beams, antennas), jnp.bfloat16),
            pltpu.VMEM((2, 2, samples, antennas), jnp.bfloat16),
            pltpu.VMEM((2,) + ((beams // per, per) if per % 8 == 0 else (beams,)) + (samples,), jnp.float32),
            pltpu.SMEM((2, tap_total), jnp.float32),
            pltpu.SemaphoreType.DMA((tiles,)),
            pltpu.SemaphoreType.DMA,
            pltpu.SemaphoreType.DMA,
            pltpu.SemaphoreType.DMA((4,)),
        ],
        compiler_params=pltpu.CompilerParams(vmem_limit_bytes=67043328),
        name="channelize",
    )(taps.T, x, w)


UNROLL = 128
RAMPS = 8


def merge_table(offsets, boxes, half, block, per):
    levels, _, delays = offsets.shape
    row = jnp.arange(delays, dtype=jnp.int32)
    parts = []
    for level in range(levels):
        child = delays >> (levels - level)
        base = row & ~(2 * child - 1)
        low, high = offsets[level, 0], offsets[level, 1]
        part = jnp.stack([(base + low) * per, (base + child + high) * per, low])
        if level == levels - 1:
            near, far = part[:, : delays // 2], part[:, delays // 2 :]
            part = jnp.where(half == 0, jnp.concatenate([near, far], 1), jnp.concatenate([far, near], 1))
        parts.append(part)
    table = jnp.stack(parts).reshape(-1)
    tail = jnp.concatenate([boxes, jnp.full((1,), block, jnp.int32)])
    return jnp.concatenate([table, jnp.pad(tail, (0, 128 - tail.shape[0]))])


def repeat(count, body):
    if count == 1:
        body(0, 0)
    else:
        lax.fori_loop(0, count, body, 0)


def split_lanes(value):
    return [value[:, 128 * t : 128 * t + 128] for t in range(value.shape[-1] // 128)]


def shifted(pieces, amount, limit):
    lane = lax.broadcasted_iota(jnp.int32, pieces[0].shape, 1)
    zero = jnp.zeros_like(pieces[0])
    tiles = len(pieces)
    rest = amount
    if limit > 128:
        whole = amount >> 7
        rest = amount & 127
        moved = []
        for t in range(tiles):
            piece = zero
            for q in range(t + 1):
                piece = jnp.where(whole == q, pieces[t - q], piece)
            moved.append(piece)
        pieces = moved
    rolled = [pltpu.roll(piece, rest, 1) for piece in pieces]
    kept = lane >= rest
    return [jnp.where(kept, rolled[t], rolled[t - 1] if t else zero) for t in range(tiles)]


def k2_kernel(
    table_hbm, normed_ref, dedispersed_ref, scores_ref, peak_ref,
    plane_a, plane_b, own, other, *rest_refs,
):
    *ramps, tops, table_ref, table_sem, out_sem = rest_refs
    planes = (plane_a, plane_b)
    channels, per, samples = normed_ref.shape
    delays = plane_a.shape[1] // per
    tiles = samples // 128
    rate = delays // channels
    levels = (table_ref.shape[0] - 128) // (3 * delays)
    half_rows = delays // 2
    box_total = scores_ref.shape[0]
    tail = 3 * delays * levels
    table_copy = pltpu.make_async_copy(table_hbm, table_ref, table_sem)
    table_copy.start()
    for ramp in ramps:
        ramp[pl.ds(0, samples), :] = jnp.zeros((samples, 128), jnp.float32)
    total = normed_ref[0]
    for c in range(1, channels):
        total = total + normed_ref[c]
    common = total * (1.0 / channels)

    group = min(4, channels)

    def put(level, t, row, value):
        rows = pl.ds(row * per if isinstance(row, int) else pl.multiple_of(row * per, per), per)
        planes[level % 2][t, rows, :] = value

    def first(i, carry):
        terms = []
        for u in range(group):
            cleaned = split_lanes(normed_ref[group * i + u] - common)
            running = cleaned
            terms.append(running)
            for lag in range(1, rate):
                running = [a + b for a, b in zip(running, shifted(cleaned, lag, 1))]
                terms.append(running)
        for u in range(group * rate):
            for t in range(tiles):
                put(0, t, group * rate * i + u, terms[u][t])
        return carry

    lax.fori_loop(0, channels // group, first, 0)
    table_copy.wait()

    def merged(level, row):
        start = 3 * delays * level
        lower = table_ref[start + row]
        upper = table_ref[start + delays + row]
        low = table_ref[start + 2 * delays + row]
        source = planes[level % 2]
        lower_rows = pl.ds(pl.multiple_of(lower, per), per)
        upper_rows = pl.ds(pl.multiple_of(upper, per), per)
        moved = shifted([source[t, upper_rows, :] for t in range(tiles)], low, rate << level)
        return [source[t, lower_rows, :] + moved[t] for t in range(tiles)]

    for level in range(levels - 1):
        def one(i, carry, level=level):
            for u in range(UNROLL):
                row = merged(level, UNROLL * i + u)
                for t in range(tiles):
                    put(level + 1, t, UNROLL * i + u, row[t])
            return carry
        repeat(delays // UNROLL, one)

    scale = 1.0 / math.sqrt(channels)
    step = 8
    span = min(UNROLL, half_rows)
    for k in range(2):
        target = own if k == 0 else other
        def last(i, carry, k=k, target=target):
            for v in range(span // step):
                place = span * i + step * v
                rows = [jnp.concatenate(merged(levels - 1, k * half_rows + place + u), 1) * scale for u in range(step)]
                if per % 8 == 0:
                    target[:, pl.ds(place if isinstance(place, int) else pl.multiple_of(place, step), step), :] = jnp.transpose(jnp.stack(rows, 0), (1, 0, 2))
                else:
                    for u in range(step):
                        for b in range(per):
                            target[b, pl.ds(place + u, 1), :] = rows[u][b : b + 1]
            return carry
        repeat(half_rows // span, last)

    out_copy = pltpu.make_async_copy(own, dedispersed_ref, out_sem)
    out_copy.start()
    width = per * half_rows
    groups = width // 128
    head = samples // 2
    later = lax.broadcasted_iota(jnp.int32, (head, head), 0)
    earlier = lax.broadcasted_iota(jnp.int32, (head, head), 1)
    upto = jnp.where(earlier <= later, 1.0, 0.0).astype(jnp.bfloat16)
    upto = jnp.concatenate([upto] * 3, 1)
    spot = lax.broadcasted_iota(jnp.int32, (box_total, 128), 0)
    lengths = jnp.zeros((box_total, 128), jnp.int32)
    for w in range(box_total):
        lengths = jnp.where(spot == w, table_ref[tail + w], lengths)
    roots = jnp.sqrt(lengths.astype(jnp.float32))
    flat = [own.reshape(width, samples), other.reshape(width, samples)]
    block_rows = 64

    def sums(g, k):
        rows = flat[k][pl.ds(128 * g, 128), :]
        rest = jnp.concatenate([rows[:, :head], rows[:, head:]], 0)
        parts = []
        for piece in range(3):
            parts.append(rest.astype(jnp.bfloat16))
            if piece < 2:
                rest = rest - parts[-1].astype(jnp.float32)
        got = lax.dot_general(
            upto, jnp.concatenate(parts, 1), (((1,), (1,)), ((), ())), preferred_element_type=jnp.float32
        )
        ramp = ramps[(2 * g + k) % len(ramps)]
        ramp[pl.ds(samples, head), :] = got[:, :128]
        ramp[pl.ds(samples + head, head), :] = got[:, 128:] + got[head - 1 :, :128]

    def boxes(g, k):
        ramp = ramps[(2 * g + k) % len(ramps)]
        best = [None] * box_total
        for s0 in range(0, samples, block_rows):
            here = ramp[pl.ds(samples + s0, block_rows), :]
            for w in range(box_total):
                response = here - ramp[pl.ds(samples + s0 - table_ref[tail + w], block_rows), :]
                found = jnp.max(response.reshape(block_rows // 8, 8, 128), axis=0)
                best[w] = found if best[w] is None else jnp.maximum(best[w], found)
        scores = jnp.concatenate([jnp.max(b, axis=0, keepdims=True) for b in best], 0) / roots
        if k == 0:
            scores_ref[:, pl.ds(128 * g, 128)] = scores
        tops[pl.ds(k * groups + g, 1), :] = jnp.max(scores, axis=0, keepdims=True)

    order = [(g, k) for k in range(2) for g in range(groups)]
    sums(*order[0])
    for n, spot_now in enumerate(order):
        if n + 1 < len(order):
            sums(*order[n + 1])
        boxes(*spot_now)
    block = table_ref[tail + box_total]
    values = tops[...]
    lane = lax.broadcasted_iota(jnp.int32, values.shape, 1)
    place = lax.broadcasted_iota(jnp.int32, values.shape, 0)
    place = 128 * jnp.where(place >= groups, place - groups, place)
    peaks = jnp.full(values.shape, -jnp.inf, jnp.float32)
    span = min(half_rows, 128)
    for q in range(128 // span):
        inside = (lane >= span * q) & (lane < span * (q + 1))
        top = jnp.max(jnp.where(inside, values, -jnp.inf), axis=1, keepdims=True)
        beam = block * per + (place + span * q) // half_rows
        peaks = jnp.where(lane == beam, jnp.maximum(top, peaks), peaks)
    peak_ref[...] = jnp.max(peaks, axis=0, keepdims=True)[:, : peak_ref.shape[1]]
    out_copy.wait()


def k2(table, normed, beams, delays, box_total):
    channels, per, samples = normed.shape
    half_rows = delays // 2
    groups = per * half_rows // 128
    vmem = pl.BlockSpec(memory_space=pltpu.VMEM)
    hbm = pl.BlockSpec(memory_space=pl.ANY)
    return pl.pallas_call(
        k2_kernel,
        out_shape=(
            jax.ShapeDtypeStruct((per, half_rows, samples), jnp.float32),
            jax.ShapeDtypeStruct((box_total, per * half_rows), jnp.float32),
            jax.ShapeDtypeStruct((1, beams), jnp.float32),
        ),
        in_specs=[hbm, vmem],
        out_specs=(hbm, vmem, vmem),
        scratch_shapes=[
            *[pltpu.VMEM((samples // 128, delays * per, 128), jnp.float32)] * 2,
            *[pltpu.VMEM((per, half_rows, samples), jnp.float32)] * 2,
            *[pltpu.VMEM((2 * samples, 128), jnp.float32)] * RAMPS,
            pltpu.VMEM((2 * groups, 128), jnp.float32),
            pltpu.SMEM(table.shape, jnp.int32),
            pltpu.SemaphoreType.DMA,
            pltpu.SemaphoreType.DMA,
        ],
        compiler_params=pltpu.CompilerParams(vmem_limit_bytes=48 << 20),
        name="dedisperse",
    )(table, normed)


def shards(voltages, pfb_taps, steering, fdmt_offsets, box_lengths):
    devices = lax.axis_size("freq")
    device_id = lax.axis_index("freq")
    beams = steering.shape[-1]
    blocks = devices // 2
    per = beams // blocks
    samples = voltages.shape[1] - pfb_taps.shape[0] + 1
    normed = k1(pfb_taps, voltages[0], steering, per)
    if normed.ndim == 3:
        normed = normed.reshape(2, blocks, per, samples).transpose(1, 0, 2, 3)
        normed = jnp.broadcast_to(normed[None], (2,) + normed.shape)
    outgoing = normed.reshape(devices, 2, per, samples)
    incoming = lax.all_to_all(outgoing, "freq", split_axis=0, concat_axis=0, tiled=True)
    table = merge_table(fdmt_offsets, box_lengths, device_id // blocks, device_id % blocks, per)
    delays, box_total = fdmt_offsets.shape[-1], box_lengths.shape[0]
    dedispersed, box_scores, peaks = k2(
        table, incoming.reshape(2 * devices, per, samples), beams, delays, box_total
    )
    box_scores = box_scores.reshape(box_total, per, delays // 2).transpose(1, 0, 2)
    steps = [1 << bit for bit in range(1, blocks.bit_length() - 1)]
    phases = [(a, b, a + b) for a, b in zip(steps[::2], steps[1::2])]
    phases += [(step,) for step in steps[len(phases) * 2 :]] + [(1,)]
    for phase in phases if blocks > 1 else []:
        arrived = [
            lax.ppermute(peaks, "freq", [(spot, spot ^ step) for spot in range(devices)]) for step in phase
        ]
        for piece in arrived:
            peaks = jnp.maximum(peaks, piece)
    return (dedispersed, box_scores, peaks.reshape(beams))


def solution(mesh):
    placed = (
        P(("groups", "freq"), None, None, None, None),
        P(),
        P(("groups", "freq"), None, None, None),
        P(),
        P(),
    )
    return jax.shard_map(
        shards,
        mesh=mesh,
        in_specs=placed,
        out_specs=(
            P(("groups", "freq"), None, None),
            P(("groups", "freq"), None, None),
            P("groups"),
        ),
        check_vma=False,
    )
```

```python
import functools
import math

import jax
import jax.numpy as jnp
from jax import lax
from jax.experimental import pallas as pl
from jax.experimental.pallas import tpu as pltpu
from jax.sharding import PartitionSpec as P


def k1_kernel(chunk, taps_hbm, x_hbm, w_hbm, out_ref, slab, wbuf, fine, taps_ref, x_sem, w_sem, taps_sem):
    branches, tap_total = taps_ref.shape
    rows_in, tiles = x_hbm.shape[0], x_hbm.shape[1]
    samples = fine.shape[2]
    beams2 = wbuf.shape[1]
    beams = beams2 // 2
    flat = slab.reshape(tiles, 2 * slab.shape[1], 128)
    window = -(-4 * (chunk + tap_total - 1) // 16) * 16

    def x_copy(j):
        return pltpu.make_async_copy(x_hbm.at[:, j], slab.at[j, pl.ds(0, rows_in)], x_sem.at[j])

    taps_copy = pltpu.make_async_copy(taps_hbm, taps_ref, taps_sem)
    taps_copy.start()
    for j in range(tiles):
        x_copy(j).start()
    w_copy = pltpu.make_async_copy(w_hbm, wbuf, w_sem)
    w_copy.start()
    taps_copy.wait()
    shape = (2, 2, chunk, window)
    col = lax.broadcasted_iota(jnp.int32, shape, 3)
    part = lax.broadcasted_iota(jnp.int32, shape, 0)
    fsel = lax.broadcasted_iota(jnp.int32, shape, 1)
    tap = (col >> 2) - lax.broadcasted_iota(jnp.int32, shape, 2)
    branch = (col >> 1) & 1
    code = jnp.where((col & 1) == part, tap * 2 + branch, -1)
    weights = jnp.zeros(shape, jnp.float32)
    for k in range(tap_total):
        for p in range(branches):
            weights = jnp.where(code == 2 * k + p, taps_ref[p, k], weights)
    weights = jnp.where((fsel & branch) == 1, -weights, weights).reshape(4 * chunk, window)
    high = weights.astype(jnp.bfloat16)
    low = (weights - high.astype(jnp.float32)).astype(jnp.bfloat16)
    spans = [(s0, min(chunk, samples - s0)) for s0 in range(0, samples, chunk)]
    spans = [(s0, size, -(-4 * (size + tap_total - 1) // 16) * 16) for s0, size in spans]
    filters = {}
    for _, size, reach in spans:
        if size not in filters:
            filters[size] = jnp.concatenate(
                [part[q * chunk : q * chunk + size, :reach] for part in (high, low) for q in range(4)], 0
            )

    def load(g, s0, size, reach):
        pieces = [flat[2 * g + i, pl.ds(4 * s0, reach), :] for i in range(2)]
        return jnp.concatenate(pieces, 1)

    def pairs(first, many):
        work = []
        for u in range(many):
            g = first + u
            work += [(g, *span) for span in spans]
        for u in range(2 * many):
            x_copy(2 * first + u).wait()
        ahead = load(*work[0])
        for n, (g, s0, size, _) in enumerate(work):
            here = ahead
            if n + 1 < len(work):
                ahead = load(*work[n + 1])
            got = jnp.dot(filters[size], here, preferred_element_type=jnp.float32)
            rounded = (got[: 4 * size] + got[4 * size :]).astype(jnp.bfloat16)
            for q in range(4):
                fine[q // 2, q % 2, pl.ds(s0, size), pl.ds(256 * g, 256)] = rounded[
                    q * size : (q + 1) * size
                ]

    for j in range(tiles):
        spare = slab.shape[1] - rows_in
        if spare:
            slab[j, pl.ds(rows_in, spare)] = jnp.zeros((spare, 2, 128), jnp.bfloat16)
    place = 0
    pair_total = tiles // 2
    for many in (1, pair_total // 2 - 1, pair_total - pair_total // 2):
        pairs(place, many)
        place += many
    w_copy.wait()
    for f in range(2):
        dims = (((1,), (1,)), ((), ()))
        got_re = lax.dot_general(fine[0, f], wbuf[f], dims, preferred_element_type=jnp.float32).T
        got_im = lax.dot_general(fine[1, f], wbuf[f], dims, preferred_element_type=jnp.float32).T
        beam_re = got_re[:beams] - got_im[beams:]
        beam_im = got_re[beams:] + got_im[:beams]
        power = beam_re * beam_re + beam_im * beam_im
        level = jnp.mean(power, axis=-1, keepdims=True)
        centered = power - level
        spread = jnp.mean(centered * centered, axis=-1, keepdims=True)
        normed = centered / jnp.sqrt(spread + 1e-05)
        if out_ref.ndim == 5:
            normed = normed.reshape(out_ref.shape[1], out_ref.shape[3], samples)
            for h in range(2):
                out_ref[h, :, f] = normed
        else:
            out_ref[f] = normed

def k1(taps, volume, steering, per):
    t, branches, parts, antennas = volume.shape
    tap_total = taps.shape[0]
    samples = t - tap_total + 1
    beams = steering.shape[-1]
    tiles = antennas // 128
    x = volume.reshape(t * 2, 2, tiles, 128).transpose(0, 2, 1, 3)
    w = steering.transpose(0, 1, 3, 2).reshape(2, 2 * beams, antennas)
    chunk = (64 - tap_total + 1) // 16 * 16
    depth = -(-4 * t // 16) * 16
    out_dims = (2, beams // per, 2, per, samples) if per % 8 == 0 else (2, beams, samples)
    return pl.pallas_call(
        functools.partial(k1_kernel, chunk),
        out_shape=jax.ShapeDtypeStruct(out_dims, jnp.float32),
        in_specs=[pl.BlockSpec(memory_space=pltpu.HBM)] * 3,
        out_specs=pl.BlockSpec(memory_space=pltpu.VMEM),
        scratch_shapes=[
            pltpu.VMEM((tiles, depth // 2, 2, 128), jnp.bfloat16),
            pltpu.VMEM((2, 2 * beams, antennas), jnp.bfloat16),
            pltpu.VMEM((2, 2, samples, antennas), jnp.bfloat16),
            pltpu.SMEM((2, tap_total), jnp.float32),
            pltpu.SemaphoreType.DMA((tiles,)),
            pltpu.SemaphoreType.DMA,
            pltpu.SemaphoreType.DMA,
        ],
        compiler_params=pltpu.CompilerParams(vmem_limit_bytes=67043328),
        name="channelize",
    )(taps.T, x, w)


UNROLL = 128
RAMPS = 8


def merge_table(offsets, boxes, half, block, per):
    levels, _, delays = offsets.shape
    row = jnp.arange(delays, dtype=jnp.int32)
    parts = []
    for level in range(levels):
        child = delays >> (levels - level)
        base = row & ~(2 * child - 1)
        low, high = offsets[level, 0], offsets[level, 1]
        part = jnp.stack([(base + low) * per, (base + child + high) * per, low])
        if level == levels - 1:
            near, far = part[:, : delays // 2], part[:, delays // 2 :]
            part = jnp.where(half == 0, jnp.concatenate([near, far], 1), jnp.concatenate([far, near], 1))
        parts.append(part)
    table = jnp.stack(parts).reshape(-1)
    tail = jnp.concatenate([boxes, jnp.full((1,), block, jnp.int32)])
    return jnp.concatenate([table, jnp.pad(tail, (0, 128 - tail.shape[0]))])


def repeat(count, body):
    if count == 1:
        body(0, 0)
    else:
        lax.fori_loop(0, count, body, 0)


def split_lanes(value):
    return [value[:, 128 * t : 128 * t + 128] for t in range(value.shape[-1] // 128)]


def shifted(pieces, amount, limit):
    lane = lax.broadcasted_iota(jnp.int32, pieces[0].shape, 1)
    zero = jnp.zeros_like(pieces[0])
    tiles = len(pieces)
    rest = amount
    if limit > 128:
        whole = amount >> 7
        rest = amount & 127
        moved = []
        for t in range(tiles):
            piece = zero
            for q in range(t + 1):
                piece = jnp.where(whole == q, pieces[t - q], piece)
            moved.append(piece)
        pieces = moved
    rolled = [pltpu.roll(piece, rest, 1) for piece in pieces]
    kept = lane >= rest
    return [jnp.where(kept, rolled[t], rolled[t - 1] if t else zero) for t in range(tiles)]


def k2_kernel(
    table_hbm, normed_ref, dedispersed_ref, scores_ref, peak_ref,
    plane_a, plane_b, own, other, *rest_refs,
):
    *ramps, tops, table_ref, table_sem, out_sem = rest_refs
    planes = (plane_a, plane_b)
    channels, per, samples = normed_ref.shape
    delays = plane_a.shape[1] // per
    tiles = samples // 128
    rate = delays // channels
    levels = (table_ref.shape[0] - 128) // (3 * delays)
    half_rows = delays // 2
    box_total = scores_ref.shape[0]
    tail = 3 * delays * levels
    table_copy = pltpu.make_async_copy(table_hbm, table_ref, table_sem)
    table_copy.start()
    for ramp in ramps:
        ramp[pl.ds(0, samples), :] = jnp.zeros((samples, 128), jnp.float32)
    total = normed_ref[0]
    for c in range(1, channels):
        total = total + normed_ref[c]
    common = total * (1.0 / channels)

    group = min(8, channels)

    def put(level, t, row, value):
        rows = pl.ds(row * per if isinstance(row, int) else pl.multiple_of(row * per, per), per)
        planes[level % 2][t, rows, :] = value

    def first(i, carry):
        terms = []
        for u in range(group):
            cleaned = split_lanes(normed_ref[group * i + u] - common)
            running = cleaned
            terms.append(running)
            for lag in range(1, rate):
                running = [a + b for a, b in zip(running, shifted(cleaned, lag, 1))]
                terms.append(running)
        for u in range(group * rate):
            for t in range(tiles):
                put(0, t, group * rate * i + u, terms[u][t])
        return carry

    lax.fori_loop(0, channels // group, first, 0)
    table_copy.wait()

    def merged(level, row):
        start = 3 * delays * level
        lower = table_ref[start + row]
        upper = table_ref[start + delays + row]
        low = table_ref[start + 2 * delays + row]
        source = planes[level % 2]
        lower_rows = pl.ds(pl.multiple_of(lower, per), per)
        upper_rows = pl.ds(pl.multiple_of(upper, per), per)
        moved = shifted([source[t, upper_rows, :] for t in range(tiles)], low, rate << level)
        return [source[t, lower_rows, :] + moved[t] for t in range(tiles)]

    for level in range(levels - 1):
        def one(i, carry, level=level):
            for u in range(UNROLL):
                row = merged(level, UNROLL * i + u)
                for t in range(tiles):
                    put(level + 1, t, UNROLL * i + u, row[t])
            return carry
        repeat(delays // UNROLL, one)

    scale = 1.0 / math.sqrt(channels)
    step = 8
    span = min(UNROLL, half_rows)
    for k in range(2):
        target = own if k == 0 else other
        def last(i, carry, k=k, target=target):
            for v in range(span // step):
                place = span * i + step * v
                rows = [jnp.concatenate(merged(levels - 1, k * half_rows + place + u), 1) * scale for u in range(step)]
                if per % 8 == 0:
                    target[:, pl.ds(place if isinstance(place, int) else pl.multiple_of(place, step), step), :] = jnp.transpose(jnp.stack(rows, 0), (1, 0, 2))
                else:
                    for u in range(step):
                        for b in range(per):
                            target[b, pl.ds(place + u, 1), :] = rows[u][b : b + 1]
            return carry
        repeat(half_rows // span, last)

    out_copy = pltpu.make_async_copy(own, dedispersed_ref, out_sem)
    out_copy.start()
    width = per * half_rows
    groups = width // 128
    head = samples // 2
    later = lax.broadcasted_iota(jnp.int32, (head, head), 0)
    earlier = lax.broadcasted_iota(jnp.int32, (head, head), 1)
    upto = jnp.where(earlier <= later, 1.0, 0.0).astype(jnp.bfloat16)
    upto = jnp.concatenate([upto] * 3, 1)
    spot = lax.broadcasted_iota(jnp.int32, (box_total, 128), 0)
    lengths = jnp.zeros((box_total, 128), jnp.int32)
    for w in range(box_total):
        lengths = jnp.where(spot == w, table_ref[tail + w], lengths)
    roots = jnp.sqrt(lengths.astype(jnp.float32))
    flat = [own.reshape(width, samples), other.reshape(width, samples)]
    block_rows = 64

    def sums(g, k):
        rows = flat[k][pl.ds(128 * g, 128), :]
        rest = jnp.concatenate([rows[:, :head], rows[:, head:]], 0)
        parts = []
        for piece in range(3):
            parts.append(rest.astype(jnp.bfloat16))
            if piece < 2:
                rest = rest - parts[-1].astype(jnp.float32)
        got = lax.dot_general(
            upto, jnp.concatenate(parts, 1), (((1,), (1,)), ((), ())), preferred_element_type=jnp.float32
        )
        ramp = ramps[(2 * g + k) % len(ramps)]
        ramp[pl.ds(samples, head), :] = got[:, :128]
        ramp[pl.ds(samples + head, head), :] = got[:, 128:] + got[head - 1 :, :128]

    def boxes(g, k):
        ramp = ramps[(2 * g + k) % len(ramps)]
        best = [None] * box_total
        for s0 in range(0, samples, block_rows):
            here = ramp[pl.ds(samples + s0, block_rows), :]
            for w in range(box_total):
                response = here - ramp[pl.ds(samples + s0 - table_ref[tail + w], block_rows), :]
                found = jnp.max(response.reshape(block_rows // 8, 8, 128), axis=0)
                best[w] = found if best[w] is None else jnp.maximum(best[w], found)
        scores = jnp.concatenate([jnp.max(b, axis=0, keepdims=True) for b in best], 0) / roots
        if k == 0:
            scores_ref[:, pl.ds(128 * g, 128)] = scores
        tops[pl.ds(k * groups + g, 1), :] = jnp.max(scores, axis=0, keepdims=True)

    order = [(g, k) for k in range(2) for g in range(groups)]
    sums(*order[0])
    for n, spot_now in enumerate(order):
        if n + 1 < len(order):
            sums(*order[n + 1])
        boxes(*spot_now)
    block = table_ref[tail + box_total]
    values = tops[...]
    lane = lax.broadcasted_iota(jnp.int32, values.shape, 1)
    place = lax.broadcasted_iota(jnp.int32, values.shape, 0)
    place = 128 * jnp.where(place >= groups, place - groups, place)
    peaks = jnp.full(values.shape, -jnp.inf, jnp.float32)
    span = min(half_rows, 128)
    for q in range(128 // span):
        inside = (lane >= span * q) & (lane < span * (q + 1))
        top = jnp.max(jnp.where(inside, values, -jnp.inf), axis=1, keepdims=True)
        beam = block * per + (place + span * q) // half_rows
        peaks = jnp.where(lane == beam, jnp.maximum(top, peaks), peaks)
    peak_ref[...] = jnp.max(peaks, axis=0, keepdims=True)[:, : peak_ref.shape[1]]
    out_copy.wait()


def k2(table, normed, beams, delays, box_total):
    channels, per, samples = normed.shape
    half_rows = delays // 2
    groups = per * half_rows // 128
    vmem = pl.BlockSpec(memory_space=pltpu.VMEM)
    hbm = pl.BlockSpec(memory_space=pl.ANY)
    return pl.pallas_call(
        k2_kernel,
        out_shape=(
            jax.ShapeDtypeStruct((per, half_rows, samples), jnp.float32),
            jax.ShapeDtypeStruct((box_total, per * half_rows), jnp.float32),
            jax.ShapeDtypeStruct((1, beams), jnp.float32),
        ),
        in_specs=[hbm, vmem],
        out_specs=(hbm, vmem, vmem),
        scratch_shapes=[
            *[pltpu.VMEM((samples // 128, delays * per, 128), jnp.float32)] * 2,
            *[pltpu.VMEM((per, half_rows, samples), jnp.float32)] * 2,
            *[pltpu.VMEM((2 * samples, 128), jnp.float32)] * RAMPS,
            pltpu.VMEM((2 * groups, 128), jnp.float32),
            pltpu.SMEM(table.shape, jnp.int32),
            pltpu.SemaphoreType.DMA,
            pltpu.SemaphoreType.DMA,
        ],
        compiler_params=pltpu.CompilerParams(vmem_limit_bytes=48 << 20),
        name="dedisperse",
    )(table, normed)


def shards(voltages, pfb_taps, steering, fdmt_offsets, box_lengths):
    devices = lax.axis_size("freq")
    device_id = lax.axis_index("freq")
    beams = steering.shape[-1]
    blocks = devices // 2
    per = beams // blocks
    samples = voltages.shape[1] - pfb_taps.shape[0] + 1
    normed = k1(pfb_taps, voltages[0], steering, per)
    if normed.ndim == 3:
        normed = normed.reshape(2, blocks, per, samples).transpose(1, 0, 2, 3)
        normed = jnp.broadcast_to(normed[None], (2,) + normed.shape)
    outgoing = normed.reshape(devices, 2, per, samples)
    incoming = lax.all_to_all(outgoing, "freq", split_axis=0, concat_axis=0, tiled=True)
    table = merge_table(fdmt_offsets, box_lengths, device_id // blocks, device_id % blocks, per)
    delays, box_total = fdmt_offsets.shape[-1], box_lengths.shape[0]
    dedispersed, box_scores, peaks = k2(
        table, incoming.reshape(2 * devices, per, samples), beams, delays, box_total
    )
    box_scores = box_scores.reshape(box_total, per, delays // 2).transpose(1, 0, 2)
    steps = [1 << bit for bit in range(1, blocks.bit_length() - 1)]
    phases = [(a, b, a + b) for a, b in zip(steps[::2], steps[1::2])]
    phases += [(step,) for step in steps[len(phases) * 2 :]] + [(1,)]
    for phase in phases if blocks > 1 else []:
        arrived = [
            lax.ppermute(peaks, "freq", [(spot, spot ^ step) for spot in range(devices)]) for step in phase
        ]
        for piece in arrived:
            peaks = jnp.maximum(peaks, piece)
    return (dedispersed, box_scores, peaks.reshape(beams))


def solution(mesh):
    placed = (
        P(("groups", "freq"), None, None, None, None),
        P(),
        P(("groups", "freq"), None, None, None),
        P(),
        P(),
    )
    return jax.shard_map(
        shards,
        mesh=mesh,
        in_specs=placed,
        out_specs=(
            P(("groups", "freq"), None, None),
            P(("groups", "freq"), None, None),
            P("groups"),
        ),
        check_vma=False,
    )
```
